256 devices in a mesh: row: 8 (over x, core), col: 32 (over z, y).
Axes of the slice: x: 4, y: 4, z: 8, core: 2. Of those that a mesh axis runs over, the one named last changes fastest.
Arguments:
- ancestor_order: int32 [2, 48], replicated, may hold values from 0 to 47, each once within a row
- factor_rows: bfloat16 [2, 24576, 512], P(None, ('row', 'col')), may hold values from -0.0390625 to 0.0390625
- factor_inverse: bfloat16 [2, 512, 512], replicated
- ancestor_inverse: bfloat16 [24576, 24576], P('col', 'row'), may hold values from -6 to 6
- diagonal_inverse: float32 [2, 512, 512], P(None, None, 'row'), may hold values from -6 to 6
Outputs:
- offdiag_inverse: bfloat16 [2, 24576, 512], P(None, 'col', 'row')
- diag_updated: float32 [2, 512, 512], P(None, None, 'row')
The draws below stay inside these ranges and needn't reach their ends.
Inputs may be any that keep to these rules, and one draw needn't show every extreme that they name: `ancestor_order`: each row lists every ancestor block once; its first 40 entries are the blocks coupled to that supernode.
All inputs are finite; a program needn't handle non-finite values.
Results may differ from the reference program's by a relative error of at most 0.011.
Values may be sent and summed in bfloat16 or wider, within the bound.
No kernel may reach another device: no remote copies, remote signals or barrier semaphores. Data moves between devices by JAX's collectives and lax.ppermute only.
A program may use at most 128 MiB of HBM per device.

```python
import math
import jax
import jax.numpy as jnp
from jax import lax

B = 512
NA = 48
NSEL = 40
NSUP = 2


def draw_factor_inverse(key, part):
    noise = jax.random.normal(key, (NSUP, B, B), jnp.float32) * (0.6 / math.sqrt(B))
    lower = jnp.tril(noise, -1) + jnp.eye(B, dtype=jnp.float32)[None, :, :]
    return lower.astype(jnp.bfloat16)


def steps_of(key, dims, cuts, low, high):
    loudness = 1.0
    for position, blocks in cuts:
        heights = jax.random.uniform(jax.random.fold_in(jax.random.fold_in(key, 6), position), (blocks,), jnp.float32, low / len(cuts), high / len(cuts))
        loudness = loudness * jnp.repeat(jnp.exp(heights), dims[position] // blocks).reshape((-1,) + (1,) * (len(dims) - 1 - position))
    return loudness


def gaussian(key, dims, width, reach, split=(), kind=jnp.bfloat16):
    entries = width * jax.random.normal(key, dims, jnp.float32)
    if split:
        entries = entries * steps_of(key, dims, split, -0.22, 0.18)
    return jnp.clip(entries, -reach, reach).astype(kind)


def setup_inputs(seed: int = 0) -> dict:
    streams_of = jax.random.split(jax.random.key(seed), 6)
    return {
        "ancestor_order": jax.vmap(lambda own: jax.random.permutation(own, NA))(jax.random.split(streams_of[0], NSUP)).reshape((NSUP, NA)).astype(jnp.int32),
        "factor_rows": gaussian(streams_of[1], (NSUP, NA * B, B), (NA * B) ** -0.5, 0.0390625, ((1, 256),)),
        "factor_inverse": draw_factor_inverse(jax.random.fold_in(streams_of[5], 71), 0),
        "ancestor_inverse": gaussian(streams_of[3], (NA * B, NA * B), 1.0, 6.0, ((0, 32), (1, 8))),
        "diagonal_inverse": gaussian(streams_of[4], (NSUP, B, B), 1.0, 6.0, ((2, 8),), jnp.float32),
    }


def reference(ancestor_order, factor_rows, factor_inverse, ancestor_inverse, diagonal_inverse):
    block_width = factor_rows.shape[2]
    chosen = ancestor_order[:, :NSEL]
    labels = jnp.arange(NA, dtype=jnp.int32)
    block_mask = jnp.any(chosen[:, :, None] == labels[None, None, :], axis=1).astype(jnp.float32)
    row_mask = jnp.repeat(block_mask, block_width, axis=1)
    offdiag_list = []
    diag_list = []
    for index in range(NSUP):
        normed = jnp.dot(factor_rows[index], factor_inverse[index], preferred_element_type=jnp.float32)
        normed = (normed * row_mask[index][:, None]).astype(jnp.bfloat16)
        product = jnp.dot(ancestor_inverse, normed, preferred_element_type=jnp.float32)
        offdiag_list.append((-(product * row_mask[index][:, None])).astype(jnp.bfloat16))
        correction = jnp.dot(normed.astype(jnp.float32).T, product, precision=lax.Precision.HIGHEST)
        diag_list.append(diagonal_inverse[index] + correction)
    return jnp.stack(offdiag_list), jnp.stack(diag_list)
```

```python
import jax
import jax.numpy as jnp
from jax import lax
from jax.sharding import Mesh
from jax.sharding import PartitionSpec as P

NSEL = 40
XS, CORES, ZS, YS = 4, 2, 8, 4
ROW = ("x", "core")
COL = ("z", "y")
ALL = ("x", "core", "z", "y")
F32 = jnp.float32
BF16 = jnp.bfloat16


def shift(array, axis, size, by):
    return lax.ppermute(array, axis, [(i, (i + by) % size) for i in range(size)])


def direct_ring(array, axis, size):
    return [array] + [shift(array, axis, size, d if d <= size // 2 else d - size) for d in range(1, size)]


def relay_ring(array, axis, size, halved):
    got = [array] + [None] * (size - 1)
    right = left = array
    for step in range(1, size // 2):
        right = shift(right, axis, size, 1)
        left = shift(left, axis, size, -1)
        got[step], got[size - step] = right, left
    if halved:
        half = array.shape[0] // 2
        got[size // 2] = jnp.concatenate(
            [shift(right[:half], axis, size, 1), shift(left[half:], axis, size, -1)], axis=0
        )
    else:
        got[size // 2] = shift(right, axis, size, 1)
    return got


def placed_by_owner(got, own, axis):
    size, width = len(got), got[0].shape[axis]
    dims = list(got[0].shape)
    dims[axis] *= size
    whole = jnp.zeros(dims, got[0].dtype)
    for d, chunk in enumerate(got):
        whole = lax.dynamic_update_slice_in_dim(whole, chunk, (own - d) % size * width, axis)
    return whole


def panel_y_then_z(piece):
    part = placed_by_owner(direct_ring(piece, "y", YS), lax.axis_index("y"), 0)
    return lax.all_gather(part, "z", axis=0, tiled=True)


def panel_z_then_y(piece):
    part = placed_by_owner(relay_ring(piece[None], "z", ZS, False), lax.axis_index("z"), 0)
    whole = placed_by_owner(
        [g[:, None] for g in relay_ring(part, "y", YS, True)], lax.axis_index("y"), 1
    )
    return whole.reshape(-1, piece.shape[-1])


def sum_over_row(tiles):
    x, core = lax.axis_index("x"), lax.axis_index("core")
    kept = lax.dynamic_index_in_dim(tiles, core, 1, keepdims=False)
    given = lax.dynamic_index_in_dim(tiles, 1 - core, 1, keepdims=False)
    pair = kept.astype(F32) + lax.ppermute(given, "core", [(0, 1), (1, 0)]).astype(F32)
    pair = lax.optimization_barrier(pair.astype(BF16))
    tile = lambda k: lax.dynamic_index_in_dim(pair, (x + k) % XS, 0, keepdims=False)
    far = tile(2)
    opposite = jnp.stack([shift(far[0], "x", XS, 2), shift(far[1], "x", XS, -2)])
    near = shift(tile(1), "x", XS, 1).astype(F32) + shift(tile(3), "x", XS, -1).astype(F32)
    return (tile(0).astype(F32) + opposite.astype(F32)) + near


def summed_by_pairs(array, axis, size):
    other = lambda k: lax.ppermute(array, axis, [(i, i ^ k) for i in range(size)]).astype(F32)
    total = array.astype(F32) + other(1)
    if size == 4:
        total = total + (other(2) + other(3))
    return lax.optimization_barrier(total.astype(BF16))


SWAP = [
    ((a * ZS + b) * YS + y, (b * ZS + a) * YS + y)
    for a in range(XS * CORES)
    for b in range(ZS)
    for y in range(YS)
]


def body(listing, pieces, factor_inv, inverse_block, diag_inv):
    piece_rows, width = pieces.shape[1:]
    row = lax.axis_index(ROW)
    col = lax.axis_index(COL)
    y = lax.axis_index("y")
    chosen = listing[:, :NSEL]

    def keep_of(first, count):
        labels = (first + jnp.arange(count, dtype=jnp.int32)) // width
        return jnp.any(chosen[:, :, None] == labels[None, None, :], axis=1).astype(F32)

    own_keep = keep_of((row * ZS * YS + col) * piece_rows, piece_rows)
    normed = jnp.einsum("srk,skj->srj", pieces, factor_inv, preferred_element_type=F32)
    normed = (normed * own_keep[:, :, None]).astype(BF16)
    panels = [panel_y_then_z(normed[0]), panel_z_then_y(normed[1])]

    rows = inverse_block.shape[0]
    slab = width // (XS * CORES)
    partial = [
        jnp.einsum("qj,pq->jp", panel, inverse_block, preferred_element_type=F32)
        .astype(BF16)
        .reshape(XS, CORES, 1, slab, rows)
        for panel in panels
    ]
    product = sum_over_row(jnp.concatenate(partial, axis=2))
    col_keep = keep_of(col * rows, rows)
    offdiag = (-(product * col_keep[:, None, :])).astype(BF16)

    turned = lax.ppermute(offdiag, ALL, SWAP)
    own_slabs = [lax.dynamic_slice_in_dim(panel, y * rows, rows, 0) for panel in panels]
    terms = jnp.stack(
        [-jnp.dot(turned[s], own_slabs[s], preferred_element_type=F32) for s in range(len(panels))]
    ).astype(BF16)
    for axis, size in (("core", CORES), ("y", YS), ("x", XS)):
        terms = summed_by_pairs(terms, axis, size)
    correction = lax.ppermute(terms, ALL, SWAP).astype(F32)
    return offdiag.transpose(0, 2, 1), diag_inv + correction.transpose(0, 2, 1)


def solution(mesh):
    torus = Mesh(mesh.devices.reshape(XS, CORES, ZS, YS), ALL)
    return jax.shard_map(
        body,
        mesh=torus,
        in_specs=(P(), P(None, ALL, None), P(), P(COL, ROW), P(None, None, ROW)),
        out_specs=(P(None, COL, ROW), P(None, None, ROW)),
        check_vma=False,
    )
```

```python
import jax
import jax.numpy as jnp
from jax import lax
from jax.sharding import Mesh
from jax.sharding import PartitionSpec as P

NSEL = 40
XS, CORES, ZS, YS = 4, 2, 8, 4
ROW = ("x", "core")
COL = ("z", "y")
ALL = ("x", "core", "z", "y")
F32 = jnp.float32
BF16 = jnp.bfloat16


def shift(array, axis, size, by):
    return lax.ppermute(array, axis, [(i, (i + by) % size) for i in range(size)])


def direct_ring(array, axis, size):
    return [array] + [shift(array, axis, size, d if d <= size // 2 else d - size) for d in range(1, size)]


def relay_ring(array, axis, size, halved):
    got = [array] + [None] * (size - 1)
    right = left = array
    for step in range(1, size // 2):
        right = shift(right, axis, size, 1)
        left = shift(left, axis, size, -1)
        got[step], got[size - step] = right, left
    if halved:
        half = array.shape[0] // 2
        got[size // 2] = jnp.concatenate(
            [shift(right[:half], axis, size, 1), shift(left[half:], axis, size, -1)], axis=0
        )
    else:
        got[size // 2] = shift(right, axis, size, 1)
    return got


def placed_by_owner(got, own, axis):
    size, width = len(got), got[0].shape[axis]
    dims = list(got[0].shape)
    dims[axis] *= size
    whole = jnp.zeros(dims, got[0].dtype)
    for d, chunk in enumerate(got):
        whole = lax.dynamic_update_slice_in_dim(whole, chunk, (own - d) % size * width, axis)
    return whole


def panel_y_then_z(piece):
    part = placed_by_owner(direct_ring(piece, "y", YS), lax.axis_index("y"), 0)
    return lax.all_gather(part, "z", axis=0, tiled=True)


def panel_z_then_y(piece):
    part = placed_by_owner(direct_ring(piece[None], "z", ZS), lax.axis_index("z"), 0)
    whole = placed_by_owner(
        [g[:, None] for g in relay_ring(part, "y", YS, True)], lax.axis_index("y"), 1
    )
    return whole.reshape(-1, piece.shape[-1])


def device(x, core, z, y):
    return ((x * CORES + core) * ZS + z) * YS + y


def to_cores(own_slabs):
    x, core, z = lax.axis_index("x"), lax.axis_index("core"), lax.axis_index("z")
    home = (x == z // CORES) & (core == z % CORES)
    total = jnp.where(home, jnp.where(core == 0, own_slabs[0], own_slabs[1]), jnp.zeros((), BF16))
    across = jnp.where(core == 0, own_slabs[1], own_slabs[0])
    pairs = lambda by, s: [
        (device(r // CORES, r % CORES, r, y), device((r // CORES + by) % XS, s, r, y))
        for r in range(ZS)
        for y in range(YS)
    ]
    for s, shifts in ((0, (1, -1, 2)), (1, (1, -1, -2))):
        for by in shifts:
            total = total + lax.ppermute(own_slabs[s], ALL, pairs(by, s))
    swapped = [
        (device(r // CORES, r % CORES, r, y), device(r // CORES, 1 - r % CORES, r, y))
        for r in range(ZS)
        for y in range(YS)
    ]
    return total + lax.ppermute(across, ALL, swapped)


def sum_over_row(partial):
    x, core = lax.axis_index("x"), lax.axis_index("core")
    moved = lax.ppermute(partial[0], "core", [(1, 0)]).astype(F32) + lax.ppermute(
        partial[1], "core", [(0, 1)]
    ).astype(F32)
    pair = jnp.where(core == 0, partial[0], partial[1]).astype(F32) + moved
    pair = lax.optimization_barrier(pair.astype(BF16))
    pair = pair.reshape(XS, -1, pair.shape[1])
    tile = lambda k: lax.dynamic_index_in_dim(pair, (x + k) % XS, 0, keepdims=False)
    far = tile(2)
    half = far.shape[0] // 2
    opposite = jnp.concatenate(
        [shift(far[:half], "x", XS, 2), shift(far[half:], "x", XS, -2)], axis=0
    )
    near = shift(tile(1), "x", XS, 1).astype(F32) + shift(tile(3), "x", XS, -1).astype(F32)
    return (tile(0).astype(F32) + opposite.astype(F32)) + near


def exchanged(array, axis, size, by):
    return lax.ppermute(array, axis, [(i, i ^ by) for i in range(size)])


def summed_over_col(array):
    y = lax.axis_index("y")
    quarters = array.reshape(YS, -1, array.shape[1])
    own = lambda k: lax.dynamic_index_in_dim(quarters, y ^ k, 0, keepdims=False)
    wide = [own(0)] + [exchanged(own(k), "y", YS, k) for k in range(1, YS)]
    wide = [w.astype(F32) for w in wide]
    part = lax.optimization_barrier(((wide[0] + wide[1]) + (wide[2] + wide[3])).astype(BF16))
    wide = [part.astype(F32)] + [exchanged(part, "z", ZS, k).astype(F32) for k in range(1, 4)]
    part = lax.optimization_barrier(((wide[0] + wide[1]) + (wide[2] + wide[3])).astype(BF16))
    part = part.astype(F32) + exchanged(part, "z", ZS, 4).astype(F32)
    part = lax.optimization_barrier(part.astype(BF16))
    whole = jnp.zeros(quarters.shape, BF16)
    for k in range(YS):
        got = part if k == 0 else exchanged(part, "y", YS, k)
        whole = lax.dynamic_update_slice_in_dim(whole, got[None], y ^ k, 0)
    return whole.reshape(array.shape)


def own_slab_of_both(array):
    core = lax.axis_index("core")
    slabs = array.reshape(CORES, -1, array.shape[1])
    kept = lax.dynamic_index_in_dim(slabs, core, 0, keepdims=False)
    given = lax.dynamic_index_in_dim(slabs, 1 - core, 0, keepdims=False)
    got = lax.ppermute(given, "core", [(0, 1), (1, 0)])
    return jnp.stack([jnp.where(core == 0, kept, got), jnp.where(core == 0, got, kept)])


def body(listing, pieces, factor_inv, inverse_block, diag_inv):
    piece_rows, width = pieces.shape[1:]
    row = lax.axis_index(ROW)
    col = lax.axis_index(COL)
    core, y = lax.axis_index("core"), lax.axis_index("y")
    chosen = listing[:, :NSEL]

    def keep_of(first, count):
        labels = (first + jnp.arange(count, dtype=jnp.int32)) // width
        return jnp.any(chosen[:, :, None] == labels[None, None, :], axis=1).astype(F32)

    own_keep = keep_of((row * ZS * YS + col) * piece_rows, piece_rows)
    normed = jnp.einsum("srk,skj->srj", pieces, factor_inv, preferred_element_type=F32)
    normed = (normed * own_keep[:, :, None]).astype(BF16)
    panels = [panel_y_then_z(normed[0]), panel_z_then_y(normed[1])]

    rows = inverse_block.shape[0]
    partial = [
        jnp.einsum("qj,pq->jp", panel, inverse_block, preferred_element_type=F32).astype(BF16)
        for panel in panels
    ]
    factor_slab = to_cores(
        [lax.dynamic_slice_in_dim(panel, y * rows, rows, 0) for panel in panels]
    )
    product = sum_over_row(partial)
    col_keep = lax.dynamic_index_in_dim(keep_of(col * rows, rows), core, 0)
    offdiag = lax.optimization_barrier((-(product * col_keep)).astype(BF16))

    term = -jnp.dot(offdiag, factor_slab, preferred_element_type=F32)
    correction = own_slab_of_both(summed_over_col(term.astype(BF16)))
    return (
        own_slab_of_both(offdiag).transpose(0, 2, 1),
        diag_inv + correction.astype(F32).transpose(0, 2, 1),
    )


def solution(mesh):
    torus = Mesh(mesh.devices.reshape(XS, CORES, ZS, YS), ALL)
    return jax.shard_map(
        body,
        mesh=torus,
        in_specs=(P(), P(None, ALL, None), P(), P(COL, ROW), P(None, None, ROW)),
        out_specs=(P(None, COL, ROW), P(None, None, ROW)),
        check_vma=False,
    )
```

```python
import jax
import jax.numpy as jnp
from jax import lax
from jax.sharding import Mesh
from jax.sharding import PartitionSpec as P

NSEL = 40
XS, CORES, ZS, YS = 4, 2, 8, 4
ROW = ("x", "core")
COL = ("z", "y")
ALL = ("x", "core", "z", "y")
F32 = jnp.float32
BF16 = jnp.bfloat16


def shift(array, axis, size, by):
    return lax.ppermute(array, axis, [(i, (i + by) % size) for i in range(size)])


def direct_ring(array, axis, size):
    return [array] + [shift(array, axis, size, d if d <= size // 2 else d - size) for d in range(1, size)]


def relay_ring(array, axis, size, halved):
    got = [array] + [None] * (size - 1)
    right = left = array
    for step in range(1, size // 2):
        right = shift(right, axis, size, 1)
        left = shift(left, axis, size, -1)
        got[step], got[size - step] = right, left
    if halved:
        half = array.shape[0] // 2
        got[size // 2] = jnp.concatenate(
            [shift(right[:half], axis, size, 1), shift(left[half:], axis, size, -1)], axis=0
        )
    else:
        got[size // 2] = shift(right, axis, size, 1)
    return got


def placed_by_owner(got, own, axis):
    size, width = len(got), got[0].shape[axis]
    dims = list(got[0].shape)
    dims[axis] *= size
    whole = jnp.zeros(dims, got[0].dtype)
    for d, chunk in enumerate(got):
        whole = lax.dynamic_update_slice_in_dim(whole, chunk, (own - d) % size * width, axis)
    return whole


def panel_y_then_z(piece):
    part = placed_by_owner(direct_ring(piece, "y", YS), lax.axis_index("y"), 0)
    return lax.all_gather(part, "z", axis=0, tiled=True)


def chunks_z_then_y(piece):
    part = placed_by_owner(relay_ring(piece[None], "z", ZS, False), lax.axis_index("z"), 0)
    return [g[:, None] for g in relay_ring(part, "y", YS, True)]


def device(x, core, z, y):
    return ((x * CORES + core) * ZS + z) * YS + y


def along_x(array, by, inward):
    pairs = []
    for core in range(CORES):
        for z in range(ZS):
            for y in range(YS):
                root = device(z // CORES, core, z, y)
                other = device((z // CORES + by) % XS, core, z, y)
                pairs.append((other, root) if inward else (root, other))
    return lax.ppermute(array, ALL, pairs)


def along_x_far(array, inward):
    half = array.shape[0] // 2
    return jnp.concatenate(
        [along_x(array[:half], 2, inward), along_x(array[half:], -2, inward)], axis=0
    )


def sum_over_row(partial):
    x, core = lax.axis_index("x"), lax.axis_index("core")
    moved = lax.ppermute(partial[0], "core", [(1, 0)]).astype(F32) + lax.ppermute(
        partial[1], "core", [(0, 1)]
    ).astype(F32)
    pair = jnp.where(core == 0, partial[0], partial[1]).astype(F32) + moved
    pair = lax.optimization_barrier(pair.astype(BF16))
    pair = pair.reshape(XS, -1, pair.shape[1])
    tile = lambda k: lax.dynamic_index_in_dim(pair, (x + k) % XS, 0, keepdims=False)
    far = tile(2)
    half = far.shape[0] // 2
    opposite = jnp.concatenate(
        [shift(far[:half], "x", XS, 2), shift(far[half:], "x", XS, -2)], axis=0
    )
    near = shift(tile(1), "x", XS, 1).astype(F32) + shift(tile(3), "x", XS, -1).astype(F32)
    return (tile(0).astype(F32) + opposite.astype(F32)) + near


def summed_over_col(array):
    shares = array.reshape(ZS * YS, -1, array.shape[1])
    mine = lax.all_to_all(shares, COL, split_axis=0, concat_axis=0, tiled=True)
    mine = mine.astype(F32).sum(axis=0).astype(BF16)
    copies = jnp.broadcast_to(mine[None], shares.shape)
    return lax.all_to_all(copies, COL, split_axis=0, concat_axis=0, tiled=True).reshape(array.shape)


def own_slab_of_both(array):
    core = lax.axis_index("core")
    slabs = array.reshape(CORES, -1, array.shape[1])
    kept = lax.dynamic_index_in_dim(slabs, core, 0, keepdims=False)
    given = lax.dynamic_index_in_dim(slabs, 1 - core, 0, keepdims=False)
    got = lax.ppermute(given, "core", [(0, 1), (1, 0)])
    return jnp.stack([jnp.where(core == 0, kept, got), jnp.where(core == 0, got, kept)])


def body(listing, pieces, factor_inv, inverse_block, diag_inv):
    piece_rows, width = pieces.shape[1:]
    row = lax.axis_index(ROW)
    col = lax.axis_index(COL)
    core, z, y = lax.axis_index("core"), lax.axis_index("z"), lax.axis_index("y")
    chosen = listing[:, :NSEL]

    def keep_of(first, count):
        labels = (first + jnp.arange(count, dtype=jnp.int32)) // width
        return jnp.any(chosen[:, :, None] == labels[None, None, :], axis=1).astype(F32)

    own_keep = keep_of((row * ZS * YS + col) * piece_rows, piece_rows)
    normed = jnp.einsum("srk,skj->srj", pieces, factor_inv, preferred_element_type=F32)
    normed = (normed * own_keep[:, :, None]).astype(BF16)
    rows = inverse_block.shape[0]

    def partial_of(panel):
        return jnp.einsum("qj,pq->jp", panel, inverse_block, preferred_element_type=F32).astype(BF16)

    chunks = chunks_z_then_y(normed[1])
    panels = [panel_y_then_z(normed[0])]
    partial = [partial_of(panels[0])]
    partial[0], chunks = lax.optimization_barrier((partial[0], chunks))
    panels.append(placed_by_owner(chunks, y, 1).reshape(panels[0].shape))
    partial.append(partial_of(panels[1]))

    slabs = [lax.dynamic_slice_in_dim(panel, y * rows, rows, 0) for panel in panels]
    across = lax.ppermute(
        jnp.where(core == 0, slabs[1], slabs[0]), "core", [(0, 1), (1, 0)]
    )
    holder = core == z % CORES
    factor_slab = jnp.where(holder, jnp.where(core == 0, slabs[0], slabs[1]), across)

    product = sum_over_row(partial)
    col_keep = lax.dynamic_index_in_dim(keep_of(col * rows, rows), core, 0)
    offdiag = lax.optimization_barrier((-(product * col_keep)).astype(BF16))

    tiles = [offdiag, along_x(offdiag, 1, True), along_x_far(offdiag, True), along_x(offdiag, -1, True)]
    terms = -jnp.dot(jnp.concatenate(tiles, axis=0), factor_slab, preferred_element_type=F32)
    terms = lax.optimization_barrier(terms.astype(BF16)).reshape(XS, -1, width)
    term = jnp.where(lax.axis_index("x") == z // CORES, terms[0], jnp.zeros((), BF16))
    term = term + along_x(terms[1], 1, False) + along_x_far(terms[2], False)
    term = term + along_x(terms[3], -1, False)
    correction = own_slab_of_both(summed_over_col(term))
    return (
        own_slab_of_both(offdiag).transpose(0, 2, 1),
        diag_inv + correction.astype(F32).transpose(0, 2, 1),
    )


def solution(mesh):
    torus = Mesh(mesh.devices.reshape(XS, CORES, ZS, YS), ALL)
    return jax.shard_map(
        body,
        mesh=torus,
        in_specs=(P(), P(None, ALL, None), P(), P(COL, ROW), P(None, None, ROW)),
        out_specs=(P(None, COL, ROW), P(None, None, ROW)),
        check_vma=False,
    )
```

```python
import jax
import jax.numpy as jnp
from jax import lax
from jax.sharding import Mesh
from jax.sharding import PartitionSpec as P

NSEL = 40
XS, CORES, ZS, YS = 4, 2, 8, 4
ROW = ("x", "core")
COL = ("z", "y")
ALL = ("x", "core", "z", "y")
F32 = jnp.float32
BF16 = jnp.bfloat16


def shift(array, axis, size, by):
    return lax.ppermute(array, axis, [(i, (i + by) % size) for i in range(size)])


def direct_ring(array, axis, size):
    return [array] + [shift(array, axis, size, d if d <= size // 2 else d - size) for d in range(1, size)]


def relay_ring(array, axis, size, halved):
    got = [array] + [None] * (size - 1)
    right = left = array
    for step in range(1, size // 2):
        right = shift(right, axis, size, 1)
        left = shift(left, axis, size, -1)
        got[step], got[size - step] = right, left
    if halved:
        half = array.shape[0] // 2
        got[size // 2] = jnp.concatenate(
            [shift(right[:half], axis, size, 1), shift(left[half:], axis, size, -1)], axis=0
        )
    else:
        got[size // 2] = shift(right, axis, size, 1)
    return got


def placed_by_owner(got, own, axis):
    size, width = len(got), got[0].shape[axis]
    dims = list(got[0].shape)
    dims[axis] *= size
    whole = jnp.zeros(dims, got[0].dtype)
    for d, chunk in enumerate(got):
        whole = lax.dynamic_update_slice_in_dim(whole, chunk, (own - d) % size * width, axis)
    return whole


def panel_y_then_z(piece):
    part = placed_by_owner(direct_ring(piece, "y", YS), lax.axis_index("y"), 0)
    return lax.all_gather(part, "z", axis=0, tiled=True)


def near_z_then_y(piece):
    part = placed_by_owner(relay_ring(piece[None], "z", ZS, False), lax.axis_index("z"), 0)[:, None]
    return [part, shift(part, "y", YS, 1), shift(part, "y", YS, -1)]


def far_chunk(near):
    half = near[0].shape[0] // 2
    right = shift(near[1][:half], "y", YS, 1)
    return jnp.concatenate([right, shift(near[2][half:], "y", YS, -1)], axis=0)


def device(x, core, z, y):
    return ((x * CORES + core) * ZS + z) * YS + y


def root_of(z):
    return z // CORES


def permuted(array, target):
    pairs = []
    for x in range(XS):
        for core in range(CORES):
            for z in range(ZS):
                for y in range(YS):
                    to = target(x, core, z, y)
                    if to is not None:
                        pairs.append((device(x, core, z, y), device(*to)))
    return lax.ppermute(array, ALL, pairs)


def to_root(array, by):
    return permuted(
        array, lambda x, c, z, y: (root_of(z), c, z, y) if x == (root_of(z) + by) % XS else None
    )


def sum_over_row(partial):
    x, core = lax.axis_index("x"), lax.axis_index("core")
    moved = lax.ppermute(partial[0], "core", [(1, 0)]).astype(F32) + lax.ppermute(
        partial[1], "core", [(0, 1)]
    ).astype(F32)
    pair = jnp.where(core == 0, partial[0], partial[1]).astype(F32) + moved
    pair = lax.optimization_barrier(pair.astype(BF16))
    pair = pair.reshape(XS, -1, pair.shape[1])
    tile = lambda k: lax.dynamic_index_in_dim(pair, (x + k) % XS, 0, keepdims=False)
    far = tile(2)
    half = far.shape[0] // 2
    opposite = jnp.concatenate(
        [shift(far[:half], "x", XS, 2), shift(far[half:], "x", XS, -2)], axis=0
    )
    near = shift(tile(1), "x", XS, 1).astype(F32) + shift(tile(3), "x", XS, -1).astype(F32)
    return (tile(0).astype(F32) + opposite.astype(F32)) + near


def exchanged(array, axis, size, by):
    return lax.ppermute(array, axis, [(i, i ^ by) for i in range(size)])


def total_of(parts):
    parts = [p.astype(F32) for p in parts]
    total = parts[0] + parts[1]
    if len(parts) == 4:
        total = total + (parts[2] + parts[3])
    return lax.optimization_barrier(total.astype(BF16))


def summed_at_roots(terms):
    z, y = lax.axis_index("z"), lax.axis_index("y")
    quarter = lambda k: lax.dynamic_index_in_dim(
        terms, ((y ^ k) - root_of(z)) % XS, 0, keepdims=False
    )
    part = total_of([quarter(0)] + [exchanged(quarter(k), "y", YS, k) for k in range(1, YS)])
    part = total_of([part, exchanged(part, "z", ZS, 1)])
    return total_of(
        [part]
        + [
            permuted(
                part,
                lambda x, c, z, y: (x ^ k, c, z ^ (CORES * k), y) if x == root_of(z) else None,
            )
            for k in range(1, XS)
        ]
    )


def spread(quarter):
    got = permuted(quarter, lambda x, c, z, y: (y, c, z, y) if x == root_of(z) else None)
    got = lax.optimization_barrier(got)
    return sum(
        [
            permuted(got, lambda x, c, z, y: (x, c, z, (y + by) % YS) if y == x else None)
            for by in (1, 2, -1)
        ],
        got,
    )


def own_slab_of_both(array):
    core = lax.axis_index("core")
    slabs = array.reshape(CORES, -1, array.shape[1])
    kept = lax.dynamic_index_in_dim(slabs, core, 0, keepdims=False)
    given = lax.dynamic_index_in_dim(slabs, 1 - core, 0, keepdims=False)
    got = lax.ppermute(given, "core", [(0, 1), (1, 0)])
    return jnp.stack([jnp.where(core == 0, kept, got), jnp.where(core == 0, got, kept)])


def body(listing, pieces, factor_inv, inverse_block, diag_inv):
    piece_rows, width = pieces.shape[1:]
    row = lax.axis_index(ROW)
    col = lax.axis_index(COL)
    core, z, y = lax.axis_index("core"), lax.axis_index("z"), lax.axis_index("y")
    chosen = listing[:, :NSEL]

    def keep_of(first, count):
        labels = (first + jnp.arange(count, dtype=jnp.int32)) // width
        return jnp.any(chosen[:, :, None] == labels[None, None, :], axis=1).astype(F32)

    own_keep = keep_of((row * ZS * YS + col) * piece_rows, piece_rows)
    normed = jnp.einsum("srk,skj->srj", pieces, factor_inv, preferred_element_type=F32)
    normed = (normed * own_keep[:, :, None]).astype(BF16)
    rows = inverse_block.shape[0]

    def partial_of(panel):
        return jnp.einsum("qj,pq->jp", panel, inverse_block, preferred_element_type=F32).astype(BF16)

    near = near_z_then_y(normed[1])
    panels = [panel_y_then_z(normed[0])]
    panels[0], near = lax.optimization_barrier((panels[0], near))
    far = far_chunk(near)
    chunks = [near[0], near[1], far, near[2]]
    partial = [partial_of(panels[0])]
    panels.append(placed_by_owner(chunks, y, 1).reshape(panels[0].shape))
    partial.append(partial_of(panels[1]))

    slabs = [lax.dynamic_slice_in_dim(panel, y * rows, rows, 0) for panel in panels]
    across = lax.ppermute(
        jnp.where(core == 0, slabs[1], slabs[0]), "core", [(0, 1), (1, 0)]
    )
    holder = core == z % CORES
    factor_slab = jnp.where(holder, jnp.where(core == 0, slabs[0], slabs[1]), across)

    product = sum_over_row(partial)
    col_keep = lax.dynamic_index_in_dim(keep_of(col * rows, rows), core, 0)
    offdiag = lax.optimization_barrier((-(product * col_keep)).astype(BF16))

    half = offdiag.shape[0] // 2
    far = jnp.concatenate([to_root(offdiag[:half], 2), to_root(offdiag[half:], -2)], axis=0)
    tiles = jnp.concatenate([offdiag, to_root(offdiag, 1), far, to_root(offdiag, -1)], axis=0)
    terms = -jnp.dot(tiles, factor_slab, preferred_element_type=F32)
    terms = lax.optimization_barrier(terms.astype(BF16)).reshape(XS, -1, width)
    correction = own_slab_of_both(spread(summed_at_roots(terms)))
    return (
        own_slab_of_both(offdiag).transpose(0, 2, 1),
        diag_inv + correction.astype(F32).transpose(0, 2, 1),
    )


def solution(mesh):
    torus = Mesh(mesh.devices.reshape(XS, CORES, ZS, YS), ALL)
    return jax.shard_map(
        body,
        mesh=torus,
        in_specs=(P(), P(None, ALL, None), P(), P(COL, ROW), P(None, None, ROW)),
        out_specs=(P(None, COL, ROW), P(None, None, ROW)),
        check_vma=False,
    )
```

```python
import jax
import jax.numpy as jnp
from jax import lax
from jax.sharding import Mesh
from jax.sharding import PartitionSpec as P

NSEL = 40
XS, CORES, ZS, YS = 4, 2, 8, 4
ROW = ("x", "core")
COL = ("z", "y")
ALL = ("x", "core", "z", "y")
F32 = jnp.float32
BF16 = jnp.bfloat16


def shift(array, axis, size, by):
    return lax.ppermute(array, axis, [(i, (i + by) % size) for i in range(size)])


def direct_ring(array, axis, size):
    return [array] + [shift(array, axis, size, d if d <= size // 2 else d - size) for d in range(1, size)]


def relay_ring(array, axis, size, halved):
    got = [array] + [None] * (size - 1)
    right = left = array
    for step in range(1, size // 2):
        right = shift(right, axis, size, 1)
        left = shift(left, axis, size, -1)
        got[step], got[size - step] = right, left
    if halved:
        half = array.shape[0] // 2
        got[size // 2] = jnp.concatenate(
            [shift(right[:half], axis, size, 1), shift(left[half:], axis, size, -1)], axis=0
        )
    else:
        got[size // 2] = shift(right, axis, size, 1)
    return got


def placed_by_owner(got, own, axis):
    size, width = len(got), got[0].shape[axis]
    dims = list(got[0].shape)
    dims[axis] *= size
    whole = jnp.zeros(dims, got[0].dtype)
    for d, chunk in enumerate(got):
        whole = lax.dynamic_update_slice_in_dim(whole, chunk, (own - d) % size * width, axis)
    return whole


def panel_y_then_z(piece):
    part = placed_by_owner(direct_ring(piece, "y", YS), lax.axis_index("y"), 0)
    return lax.all_gather(part, "z", axis=0, tiled=True)


def near_z_then_y(piece):
    part = placed_by_owner(relay_ring(piece[None], "z", ZS, False), lax.axis_index("z"), 0)[:, None]
    return [part, shift(part, "y", YS, 1), shift(part, "y", YS, -1)]


def far_chunk(near):
    half = near[0].shape[0] // 2
    right = shift(near[1][:half], "y", YS, 1)
    return jnp.concatenate([right, shift(near[2][half:], "y", YS, -1)], axis=0)


def device(x, core, z, y):
    return ((x * CORES + core) * ZS + z) * YS + y


def root_of(z):
    return z // CORES, z % CORES


def from_root(array, target):
    pairs = []
    for z in range(ZS):
        for y in range(YS):
            x, core = root_of(z)
            pairs.append((device(x, core, z, y), device(*target(x, core, z, y))))
    return lax.ppermute(array, ALL, pairs)


def along_x(slab, core, shifts):
    return sum(from_root(slab, lambda x, c, z, y: ((x + by) % XS, core, z, y)) for by in shifts)


def pair_sum(partial):
    first = lax.axis_index("core") == 0
    given = lax.ppermute(jnp.where(first, partial[1], partial[0]), "core", [(0, 1), (1, 0)])
    pair = jnp.where(first, partial[0], partial[1]).astype(F32) + given.astype(F32)
    return pair.astype(BF16)


def sum_over_x(pair):
    x = lax.axis_index("x")
    pair = pair.reshape(XS, -1, pair.shape[1])
    tile = lambda k: lax.dynamic_index_in_dim(pair, (x + k) % XS, 0, keepdims=False)
    far = tile(2)
    half = far.shape[0] // 2
    opposite = jnp.concatenate(
        [shift(far[:half], "x", XS, 2), shift(far[half:], "x", XS, -2)], axis=0
    )
    near = shift(tile(1), "x", XS, 1).astype(F32) + shift(tile(3), "x", XS, -1).astype(F32)
    return (tile(0).astype(F32) + opposite.astype(F32)) + near


def exchanged(array, axis, size, by):
    return lax.ppermute(array, axis, [(i, i ^ by) for i in range(size)])


def summed_over_col(array):
    y = lax.axis_index("y")
    quarters = array.reshape(YS, -1, array.shape[1])
    own = lambda k: lax.dynamic_index_in_dim(quarters, y ^ k, 0, keepdims=False)
    part = own(0).astype(F32)
    for k in range(1, YS):
        part = part + exchanged(own(k), "y", YS, k).astype(F32)
    part = lax.optimization_barrier(part.astype(BF16))
    copies = jnp.broadcast_to(part[None], (ZS, *part.shape))
    part = lax.all_to_all(copies, "z", split_axis=0, concat_axis=0, tiled=True)
    part = lax.optimization_barrier(part.astype(F32).sum(axis=0).astype(BF16))
    whole = jnp.zeros(quarters.shape, BF16)
    for k in range(YS):
        got = part if k == 0 else exchanged(part, "y", YS, k)
        whole = lax.dynamic_update_slice_in_dim(whole, got[None], y ^ k, 0)
    return whole.reshape(array.shape)


def own_slab_of_both(array):
    core = lax.axis_index("core")
    slabs = array.reshape(CORES, -1, array.shape[1])
    kept = lax.dynamic_index_in_dim(slabs, core, 0, keepdims=False)
    given = lax.dynamic_index_in_dim(slabs, 1 - core, 0, keepdims=False)
    got = lax.ppermute(given, "core", [(0, 1), (1, 0)])
    return jnp.stack([jnp.where(core == 0, kept, got), jnp.where(core == 0, got, kept)])


def body(listing, pieces, factor_inv, inverse_block, diag_inv):
    piece_rows, width = pieces.shape[1:]
    row = lax.axis_index(ROW)
    col = lax.axis_index(COL)
    core, z, y = lax.axis_index("core"), lax.axis_index("z"), lax.axis_index("y")
    chosen = listing[:, :NSEL]

    def keep_of(first, count):
        labels = (first + jnp.arange(count, dtype=jnp.int32)) // width
        return jnp.any(chosen[:, :, None] == labels[None, None, :], axis=1).astype(F32)

    own_keep = keep_of((row * ZS * YS + col) * piece_rows, piece_rows)
    normed = jnp.einsum("srk,skj->srj", pieces, factor_inv, preferred_element_type=F32)
    normed = (normed * own_keep[:, :, None]).astype(BF16)
    rows = inverse_block.shape[0]

    def partial_of(panel):
        return jnp.einsum("qj,pq->jp", panel, inverse_block, preferred_element_type=F32).astype(BF16)

    first = core == 0
    near = near_z_then_y(normed[1])

    deep = rows // (piece_rows * YS)
    of_slab = lambda part, lane: lax.dynamic_slice_in_dim(part, lane * deep, deep, 0)
    far_part = from_root(
        of_slab(near[0], (y + 2) % YS), lambda x, c, z, y: (x, c, z, (y + 2) % YS)
    )
    slab_parts = [of_slab(near[0], y), of_slab(near[1], y), far_part, of_slab(near[2], y)]
    slab_1 = placed_by_owner(slab_parts, y, 1).reshape(rows, width)
    sent_1 = along_x(slab_1, 1, (1, -1, -2))

    panel_0 = panel_y_then_z(normed[0])
    panel_0, near = lax.optimization_barrier((panel_0, near))
    chunks = [near[0], near[1], far_chunk(near), near[2]]
    slab_0 = lax.dynamic_slice_in_dim(panel_0, y * rows, rows, 0)
    sent_0 = along_x(slab_0, 0, (1, -1, 2))
    partial = [partial_of(panel_0)]

    chunks, partial[0] = lax.optimization_barrier((chunks, partial[0]))
    across = from_root(
        jnp.where(first, slab_1, slab_0), lambda x, c, z, y: (x, 1 - c, z, y)
    )
    partial.append(partial_of(placed_by_owner(chunks, y, 1).reshape(panel_0.shape)))

    home = row == z
    factor_slab = jnp.where(home, jnp.where(first, slab_0, slab_1), sent_0 + sent_1 + across)
    pair, factor_slab = lax.optimization_barrier((pair_sum(partial), factor_slab))
    product = sum_over_x(pair)
    col_keep = lax.dynamic_index_in_dim(keep_of(col * rows, rows), core, 0)
    offdiag = lax.optimization_barrier((-(product * col_keep)).astype(BF16))

    term = -jnp.dot(offdiag, factor_slab, preferred_element_type=F32)
    correction = own_slab_of_both(summed_over_col(term.astype(BF16)))
    return (
        own_slab_of_both(offdiag).transpose(0, 2, 1),
        diag_inv + correction.astype(F32).transpose(0, 2, 1),
    )


def solution(mesh):
    torus = Mesh(mesh.devices.reshape(XS, CORES, ZS, YS), ALL)
    return jax.shard_map(
        body,
        mesh=torus,
        in_specs=(P(), P(None, ALL, None), P(), P(COL, ROW), P(None, None, ROW)),
        out_specs=(P(None, COL, ROW), P(None, None, ROW)),
        check_vma=False,
    )
```

```python
import jax
import jax.numpy as jnp
from jax import lax
from jax.sharding import Mesh
from jax.sharding import PartitionSpec as P

NSEL = 40
XS, CORES, ZS, YS = 4, 2, 8, 4
ROW = ("x", "core")
COL = ("z", "y")
ALL = ("x", "core", "z", "y")
F32 = jnp.float32
BF16 = jnp.bfloat16


def shift(array, axis, size, by):
    return lax.ppermute(array, axis, [(i, (i + by) % size) for i in range(size)])


def direct_ring(array, axis, size):
    return [array] + [shift(array, axis, size, d if d <= size // 2 else d - size) for d in range(1, size)]


def relay_ring(array, axis, size):
    got = [array] + [None] * (size - 1)
    right = left = array
    for step in range(1, size // 2):
        right = shift(right, axis, size, 1)
        left = shift(left, axis, size, -1)
        got[step], got[size - step] = right, left
    got[size // 2] = shift(right, axis, size, 1)
    return got


def placed_by_owner(got, own, axis):
    size, width = len(got), got[0].shape[axis]
    dims = list(got[0].shape)
    dims[axis] *= size
    whole = jnp.zeros(dims, got[0].dtype)
    for d, chunk in enumerate(got):
        whole = lax.dynamic_update_slice_in_dim(whole, chunk, (own - d) % size * width, axis)
    return whole


def panel_y_then_z(piece):
    part = placed_by_owner(direct_ring(piece, "y", YS), lax.axis_index("y"), 0)
    return lax.all_gather(part, "z", axis=0, tiled=True)


def near_of(part):
    return [part, shift(part, "y", YS, 1), shift(part, "y", YS, -1)]


def far_chunk(near):
    half = near[0].shape[0] // 2
    right = shift(near[1][:half], "y", YS, 1)
    return jnp.concatenate([right, shift(near[2][half:], "y", YS, -1)], axis=0)


def device(x, core, z, y):
    return ((x * CORES + core) * ZS + z) * YS + y


def root_of(z):
    return z // CORES, z % CORES


def from_root(array, target):
    pairs = []
    for z in range(ZS):
        for y in range(YS):
            x, core = root_of(z)
            to = target(x, core, z, y)
            if to is not None:
                pairs.append((device(x, core, z, y), device(*to)))
    return lax.ppermute(array, ALL, pairs)


def along_x(slab, core, shifts):
    sent = [from_root(slab, lambda x, c, z, y: ((x + by) % XS, core, z, y)) for by in shifts]
    return sent + [from_root(slab, lambda x, c, z, y: (x, core, z, y) if c != core else None)]


def sum_over_x(pair):
    x = lax.axis_index("x")
    pair = pair.reshape(XS, -1, pair.shape[1])
    tile = lambda k: lax.dynamic_index_in_dim(pair, (x + k) % XS, 0, keepdims=False)
    far = tile(2)
    half = far.shape[0] // 2
    opposite = jnp.concatenate(
        [shift(far[:half], "x", XS, 2), shift(far[half:], "x", XS, -2)], axis=0
    )
    near = shift(tile(1), "x", XS, 1).astype(F32) + shift(tile(3), "x", XS, -1).astype(F32)
    return (tile(0).astype(F32) + opposite.astype(F32)) + near


def exchanged(array, axis, size, by):
    return lax.ppermute(array, axis, [(i, i ^ by) for i in range(size)])


def summed_over_col(array):
    y = lax.axis_index("y")
    quarters = array.reshape(YS, -1, array.shape[1])
    own = lambda k: lax.dynamic_index_in_dim(quarters, y ^ k, 0, keepdims=False)
    part = own(0).astype(F32)
    for k in range(1, YS):
        part = part + exchanged(own(k), "y", YS, k).astype(F32)
    part = lax.optimization_barrier(part.astype(BF16))
    copies = jnp.broadcast_to(part[None], (ZS, *part.shape))
    part = lax.all_to_all(copies, "z", split_axis=0, concat_axis=0, tiled=True)
    part = lax.optimization_barrier(part.astype(F32).sum(axis=0).astype(BF16))
    whole = jnp.zeros(quarters.shape, BF16)
    for k in range(YS):
        got = part if k == 0 else exchanged(part, "y", YS, k)
        whole = lax.dynamic_update_slice_in_dim(whole, got[None], y ^ k, 0)
    return whole.reshape(array.shape)


def own_slab_of_both(array):
    core = lax.axis_index("core")
    slabs = array.reshape(CORES, -1, array.shape[1])
    kept = lax.dynamic_index_in_dim(slabs, core, 0, keepdims=False)
    given = lax.dynamic_index_in_dim(slabs, 1 - core, 0, keepdims=False)
    got = lax.ppermute(given, "core", [(0, 1), (1, 0)])
    return jnp.stack([jnp.where(core == 0, kept, got), jnp.where(core == 0, got, kept)])


def body(listing, pieces, factor_inv, inverse_block, diag_inv):
    piece_rows, width = pieces.shape[1:]
    row = lax.axis_index(ROW)
    col = lax.axis_index(COL)
    core, z, y = lax.axis_index("core"), lax.axis_index("z"), lax.axis_index("y")
    chosen = listing[:, :NSEL]

    def keep_of(first, count):
        labels = (first + jnp.arange(count, dtype=jnp.int32)) // width
        return jnp.any(chosen[:, :, None] == labels[None, None, :], axis=1).astype(F32)

    own_keep = keep_of((row * ZS * YS + col) * piece_rows, piece_rows)
    normed = jnp.einsum("srk,skj->srj", pieces, factor_inv, preferred_element_type=F32)
    normed = (normed * own_keep[:, :, None]).astype(BF16)
    rows = inverse_block.shape[0]

    def partial_of(panel):
        return jnp.einsum("qj,pq->jp", panel, inverse_block, preferred_element_type=F32).astype(BF16)

    ring = relay_ring(normed[1][None], "z", ZS)
    normed_0, ring[1], ring[ZS - 1] = lax.optimization_barrier((normed[0], ring[1], ring[ZS - 1]))
    panel_0 = panel_y_then_z(normed_0)

    near = near_of(placed_by_owner(ring, z, 0)[:, None])
    chunks = [near[0], near[1], far_chunk(near), near[2]]
    deep = rows // (piece_rows * YS)
    of_slab = lambda part, lane: lax.dynamic_slice_in_dim(part, lane * deep, deep, 0)
    far_part = from_root(
        of_slab(near[0], (y + 2) % YS), lambda x, c, z, y: (x, c, z, (y + 2) % YS)
    )
    slab_parts = [of_slab(near[0], y), of_slab(near[1], y), far_part, of_slab(near[2], y)]
    slab_1 = placed_by_owner(slab_parts, y, 1).reshape(rows, width)
    zero = jnp.zeros((), BF16)
    home = row == z
    factor_slab = sum(along_x(slab_1, 1, (1, -1, -2)), jnp.where(home & (core == 1), slab_1, zero))
    partial_1 = partial_of(placed_by_owner(chunks, y, 1).reshape(panel_0.shape))
    given_1 = lax.ppermute(partial_1, "core", [(0, 1)])

    panel_0, factor_slab, given_1 = lax.optimization_barrier((panel_0, factor_slab, given_1))
    slab_0 = lax.dynamic_slice_in_dim(panel_0, y * rows, rows, 0)
    sent_0 = along_x(slab_0, 0, (1, -1, 2))
    partial_0 = partial_of(panel_0)
    near_0, far_0 = [*sent_0[:2], sent_0[3]], sent_0[2]
    partial_0, near_0 = lax.optimization_barrier((partial_0, near_0))
    given_0 = lax.ppermute(partial_0, "core", [(1, 0)])

    pair = jnp.where(core == 0, partial_0, partial_1).astype(F32)
    pair = (pair + (given_0.astype(F32) + given_1.astype(F32))).astype(BF16)
    pair, far_0 = lax.optimization_barrier((pair, far_0))
    factor_slab = sum([*near_0, far_0], factor_slab + jnp.where(home & (core == 0), slab_0, zero))
    product = sum_over_x(pair)
    col_keep = lax.dynamic_index_in_dim(keep_of(col * rows, rows), core, 0)
    offdiag = lax.optimization_barrier((-(product * col_keep)).astype(BF16))

    term = -jnp.dot(offdiag, factor_slab, preferred_element_type=F32)
    correction = own_slab_of_both(summed_over_col(term.astype(BF16)))
    return (
        own_slab_of_both(offdiag).transpose(0, 2, 1),
        diag_inv + correction.astype(F32).transpose(0, 2, 1),
    )


def solution(mesh):
    torus = Mesh(mesh.devices.reshape(XS, CORES, ZS, YS), ALL)
    return jax.shard_map(
        body,
        mesh=torus,
        in_specs=(P(), P(None, ALL, None), P(), P(COL, ROW), P(None, None, ROW)),
        out_specs=(P(None, COL, ROW), P(None, None, ROW)),
        check_vma=False,
    )
```

```python
import jax
import jax.numpy as jnp
from jax import lax
from jax.sharding import Mesh
from jax.sharding import PartitionSpec as P

NSEL = 40
XS, CORES, ZS, YS = 4, 2, 8, 4
ROW = ("x", "core")
COL = ("z", "y")
ALL = ("x", "core", "z", "y")
F32 = jnp.float32
BF16 = jnp.bfloat16


def shift(array, axis, size, by):
    return lax.ppermute(array, axis, [(i, (i + by) % size) for i in range(size)])


def direct_ring(array, axis, size):
    return [array] + [shift(array, axis, size, d if d <= size // 2 else d - size) for d in range(1, size)]


def placed_by_owner(got, own, axis):
    size, width = len(got), got[0].shape[axis]
    dims = list(got[0].shape)
    dims[axis] *= size
    whole = jnp.zeros(dims, got[0].dtype)
    for d, chunk in enumerate(got):
        whole = lax.dynamic_update_slice_in_dim(whole, chunk, (own - d) % size * width, axis)
    return whole


def copies_to(array, axis, size):
    copies = jnp.broadcast_to(array[None], (size, *array.shape))
    return lax.all_to_all(copies, axis, split_axis=0, concat_axis=0, tiled=True)


def near_of(part):
    return [part, shift(part, "y", YS, 1), shift(part, "y", YS, -1)]


def far_chunk(near):
    half = near[0].shape[0] // 2
    right = shift(near[1][:half], "y", YS, 1)
    return jnp.concatenate([right, shift(near[2][half:], "y", YS, -1)], axis=0)


def device(x, core, z, y):
    return ((x * CORES + core) * ZS + z) * YS + y


def root_of(z):
    return z // CORES, z % CORES


def from_root(array, target):
    pairs = []
    for z in range(ZS):
        for y in range(YS):
            x, core = root_of(z)
            to = target(x, core, z, y)
            if to is not None:
                pairs.append((device(x, core, z, y), device(*to)))
    return lax.ppermute(array, ALL, pairs)


def moved_home(part, half):
    pairs = []
    for z in range(ZS):
        for y in range(YS):
            x, core = root_of(z)
            pairs.append((device(x, core, 2 * y + half, y), device(x, core, z, y)))
    return lax.ppermute(part, ALL, pairs)


def along_x(slab, core, shifts):
    sent = [from_root(slab, lambda x, c, z, y: ((x + by) % XS, core, z, y)) for by in shifts]
    return sent + [from_root(slab, lambda x, c, z, y: (x, core, z, y) if c != core else None)]


def sum_over_x(pair):
    x = lax.axis_index("x")
    pair = pair.reshape(XS, -1, pair.shape[1])
    tile = lambda k: lax.dynamic_index_in_dim(pair, (x + k) % XS, 0, keepdims=False)
    far = tile(2)
    half = far.shape[0] // 2
    opposite = jnp.concatenate(
        [shift(far[:half], "x", XS, 2), shift(far[half:], "x", XS, -2)], axis=0
    )
    near = shift(tile(1), "x", XS, 1).astype(F32) + shift(tile(3), "x", XS, -1).astype(F32)
    return (tile(0).astype(F32) + opposite.astype(F32)) + near


def exchanged(array, axis, size, by):
    return lax.ppermute(array, axis, [(i, i ^ by) for i in range(size)])


def summed_over_col(array):
    y = lax.axis_index("y")
    quarters = array.reshape(YS, -1, array.shape[1])
    own = lambda k: lax.dynamic_index_in_dim(quarters, y ^ k, 0, keepdims=False)
    part = own(0).astype(F32)
    for k in range(1, YS):
        part = part + exchanged(own(k), "y", YS, k).astype(F32)
    part = lax.optimization_barrier(part.astype(BF16))
    copies = jnp.broadcast_to(part[None], (ZS, *part.shape))
    part = lax.all_to_all(copies, "z", split_axis=0, concat_axis=0, tiled=True)
    part = lax.optimization_barrier(part.astype(F32).sum(axis=0).astype(BF16))
    whole = jnp.zeros(quarters.shape, BF16)
    for k in range(YS):
        got = part if k == 0 else exchanged(part, "y", YS, k)
        whole = lax.dynamic_update_slice_in_dim(whole, got[None], y ^ k, 0)
    return whole.reshape(array.shape)


def own_slab_of_both(array):
    core = lax.axis_index("core")
    slabs = array.reshape(CORES, -1, array.shape[1])
    kept = lax.dynamic_index_in_dim(slabs, core, 0, keepdims=False)
    given = lax.dynamic_index_in_dim(slabs, 1 - core, 0, keepdims=False)
    got = lax.ppermute(given, "core", [(0, 1), (1, 0)])
    return jnp.stack([jnp.where(core == 0, kept, got), jnp.where(core == 0, got, kept)])


def body(listing, pieces, factor_inv, inverse_block, diag_inv):
    piece_rows, width = pieces.shape[1:]
    row = lax.axis_index(ROW)
    col = lax.axis_index(COL)
    core, z, y = lax.axis_index("core"), lax.axis_index("z"), lax.axis_index("y")
    chosen = listing[:, :NSEL]

    def keep_of(first, count):
        labels = (first + jnp.arange(count, dtype=jnp.int32)) // width
        return jnp.any(chosen[:, :, None] == labels[None, None, :], axis=1).astype(F32)

    own_keep = keep_of((row * ZS * YS + col) * piece_rows, piece_rows)
    normed = jnp.einsum("srk,skj->srj", pieces, factor_inv, preferred_element_type=F32)
    normed = (normed * own_keep[:, :, None]).astype(BF16)
    rows = inverse_block.shape[0]

    def partial_of(panel):
        return jnp.einsum("qj,pq->jp", panel, inverse_block, preferred_element_type=F32).astype(BF16)

    zero = jnp.zeros((), BF16)
    home = row == z
    part_0 = placed_by_owner(direct_ring(normed[0], "y", YS), y, 0)
    panel_0 = lax.all_gather(part_0, "z", axis=0, tiled=True)
    near = near_of(copies_to(normed[1], "z", ZS)[:, None])

    slab_0 = jnp.concatenate([moved_home(part_0, half) for half in range(2)], axis=0)
    factor_slab = sum(along_x(slab_0, 0, (1, -1, 2)), jnp.where(home & (core == 0), slab_0, zero))
    near, factor_slab = lax.optimization_barrier((near, factor_slab))
    chunks = [near[0], near[1], far_chunk(near), near[2]]
    deep = rows // (piece_rows * YS)
    of_slab = lambda part, lane: lax.dynamic_slice_in_dim(part, lane * deep, deep, 0)
    far_part = from_root(
        of_slab(near[0], (y + 2) % YS), lambda x, c, z, y: (x, c, z, (y + 2) % YS)
    )
    slab_parts = [of_slab(near[0], y), of_slab(near[1], y), far_part, of_slab(near[2], y)]
    slab_1 = placed_by_owner(slab_parts, y, 1).reshape(rows, width)
    factor_slab = sum(
        along_x(slab_1, 1, (1, -1, -2)),
        factor_slab + jnp.where(home & (core == 1), slab_1, zero),
    )
    partial_1 = partial_of(placed_by_owner(chunks, y, 1).reshape((-1, width)))
    given_1 = lax.ppermute(partial_1, "core", [(0, 1)])

    panel_0, factor_slab, given_1 = lax.optimization_barrier((panel_0, factor_slab, given_1))
    partial_0 = partial_of(panel_0)
    given_0 = lax.ppermute(partial_0, "core", [(1, 0)])
    pair = jnp.where(core == 0, partial_0, partial_1).astype(F32)
    pair = (pair + (given_0.astype(F32) + given_1.astype(F32))).astype(BF16)
    pair = lax.optimization_barrier(pair)
    product = sum_over_x(pair)
    col_keep = lax.dynamic_index_in_dim(keep_of(col * rows, rows), core, 0)
    offdiag = lax.optimization_barrier((-(product * col_keep)).astype(BF16))

    term = -jnp.dot(offdiag, factor_slab, preferred_element_type=F32)
    correction = own_slab_of_both(summed_over_col(term.astype(BF16)))
    return (
        own_slab_of_both(offdiag).transpose(0, 2, 1),
        diag_inv + correction.astype(F32).transpose(0, 2, 1),
    )


def solution(mesh):
    torus = Mesh(mesh.devices.reshape(XS, CORES, ZS, YS), ALL)
    return jax.shard_map(
        body,
        mesh=torus,
        in_specs=(P(), P(None, ALL, None), P(), P(COL, ROW), P(None, None, ROW)),
        out_specs=(P(None, COL, ROW), P(None, None, ROW)),
        check_vma=False,
    )
```

```python
import jax
import jax.numpy as jnp
from jax import lax
from jax.sharding import Mesh
from jax.sharding import PartitionSpec as P

NSEL = 40
XS, CORES, ZS, YS = 4, 2, 8, 4
ROW = ("x", "core")
COL = ("z", "y")
ALL = ("x", "core", "z", "y")
F32 = jnp.float32
BF16 = jnp.bfloat16


def shift(array, axis, size, by):
    return lax.ppermute(array, axis, [(i, (i + by) % size) for i in range(size)])


def direct_ring(array, axis, size):
    return [array] + [shift(array, axis, size, d if d <= size // 2 else d - size) for d in range(1, size)]


def relay_ring(array, axis, size, halved):
    got = [array] + [None] * (size - 1)
    right = left = array
    for step in range(1, size // 2):
        right = shift(right, axis, size, 1)
        left = shift(left, axis, size, -1)
        got[step], got[size - step] = right, left
    if halved:
        half = array.shape[0] // 2
        got[size // 2] = jnp.concatenate(
            [shift(right[:half], axis, size, 1), shift(left[half:], axis, size, -1)], axis=0
        )
    else:
        got[size // 2] = shift(right, axis, size, 1)
    return got


def placed_by_owner(got, own, axis):
    size, width = len(got), got[0].shape[axis]
    dims = list(got[0].shape)
    dims[axis] *= size
    whole = jnp.zeros(dims, got[0].dtype)
    for d, chunk in enumerate(got):
        whole = lax.dynamic_update_slice_in_dim(whole, chunk, (own - d) % size * width, axis)
    return whole


def panel_y_then_z(piece):
    part = placed_by_owner(direct_ring(piece, "y", YS), lax.axis_index("y"), 0)
    return lax.all_gather(part, "z", axis=0, tiled=True)


def near_z_then_y(piece):
    part = placed_by_owner(relay_ring(piece[None], "z", ZS, False), lax.axis_index("z"), 0)[:, None]
    return [part, shift(part, "y", YS, 1), shift(part, "y", YS, -1)]


def far_chunk(near):
    half = near[0].shape[0] // 2
    right = shift(near[1][:half], "y", YS, 1)
    return jnp.concatenate([right, shift(near[2][half:], "y", YS, -1)], axis=0)


def device(x, core, z, y):
    return ((x * CORES + core) * ZS + z) * YS + y


def root_of(z):
    return z // CORES, z % CORES


def from_root(array, target):
    pairs = []
    for z in range(ZS):
        for y in range(YS):
            x, core = root_of(z)
            pairs.append((device(x, core, z, y), device(*target(x, core, z, y))))
    return lax.ppermute(array, ALL, pairs)


def along_x(slab, core, shifts):
    return [from_root(slab, lambda x, c, z, y: ((x + by) % XS, core, z, y)) for by in shifts]


def pair_sum(partial):
    first = lax.axis_index("core") == 0
    given = lax.ppermute(jnp.where(first, partial[1], partial[0]), "core", [(0, 1), (1, 0)])
    pair = jnp.where(first, partial[0], partial[1]).astype(F32) + given.astype(F32)
    return pair.astype(BF16)


def sum_over_x(pair):
    x = lax.axis_index("x")
    pair = pair.reshape(XS, -1, pair.shape[1])
    tile = lambda k: lax.dynamic_index_in_dim(pair, (x + k) % XS, 0, keepdims=False)
    opposite = shift(tile(2), "x", XS, 2)
    near = shift(tile(1), "x", XS, 1).astype(F32) + shift(tile(3), "x", XS, -1).astype(F32)
    return (tile(0).astype(F32) + opposite.astype(F32)) + near


def exchanged(array, axis, size, by):
    return lax.ppermute(array, axis, [(i, i ^ by) for i in range(size)])


def summed_over_col(array):
    y = lax.axis_index("y")
    quarters = array.reshape(YS, -1, array.shape[1])
    own = lambda k: lax.dynamic_index_in_dim(quarters, y ^ k, 0, keepdims=False)
    part = own(0).astype(F32)
    for k in range(1, YS):
        part = part + exchanged(own(k), "y", YS, k).astype(F32)
    part = lax.optimization_barrier(part.astype(BF16))
    copies = jnp.broadcast_to(part[None], (ZS, *part.shape))
    part = lax.all_to_all(copies, "z", split_axis=0, concat_axis=0, tiled=True)
    part = lax.optimization_barrier(part.astype(F32).sum(axis=0).astype(BF16))
    whole = jnp.zeros(quarters.shape, BF16)
    for k in range(YS):
        got = part if k == 0 else exchanged(part, "y", YS, k)
        whole = lax.dynamic_update_slice_in_dim(whole, got[None], y ^ k, 0)
    return whole.reshape(array.shape)


def own_slab_of_both(array):
    core = lax.axis_index("core")
    slabs = array.reshape(CORES, -1, array.shape[1])
    kept = lax.dynamic_index_in_dim(slabs, core, 0, keepdims=False)
    given = lax.dynamic_index_in_dim(slabs, 1 - core, 0, keepdims=False)
    got = lax.ppermute(given, "core", [(0, 1), (1, 0)])
    return jnp.stack([jnp.where(core == 0, kept, got), jnp.where(core == 0, got, kept)])


def body(listing, pieces, factor_inv, inverse_block, diag_inv):
    piece_rows, width = pieces.shape[1:]
    row = lax.axis_index(ROW)
    col = lax.axis_index(COL)
    core, z, y = lax.axis_index("core"), lax.axis_index("z"), lax.axis_index("y")
    chosen = listing[:, :NSEL]

    def keep_of(first, count):
        labels = (first + jnp.arange(count, dtype=jnp.int32)) // width
        return jnp.any(chosen[:, :, None] == labels[None, None, :], axis=1).astype(F32)

    own_keep = keep_of((row * ZS * YS + col) * piece_rows, piece_rows)
    normed = jnp.einsum("srk,skj->srj", pieces, factor_inv, preferred_element_type=F32)
    normed = (normed * own_keep[:, :, None]).astype(BF16)
    rows = inverse_block.shape[0]

    def partial_of(panel):
        return jnp.einsum("qj,pq->jp", panel, inverse_block, preferred_element_type=F32).astype(BF16)

    first = core == 0
    near = near_z_then_y(normed[1])

    deep = rows // (piece_rows * YS)
    of_slab = lambda part, lane: lax.dynamic_slice_in_dim(part, lane * deep, deep, 0)
    far_part = from_root(
        of_slab(near[0], (y + 2) % YS), lambda x, c, z, y: (x, c, z, (y + 2) % YS)
    )
    slab_parts = [of_slab(near[0], y), of_slab(near[1], y), far_part, of_slab(near[2], y)]
    slab_1 = placed_by_owner(slab_parts, y, 1).reshape(rows, width)
    sent_1 = along_x(slab_1, 1, (1, -1, -2))

    panel_0 = panel_y_then_z(normed[0])
    panel_0, near = lax.optimization_barrier((panel_0, near))
    chunks = [near[0], near[1], far_chunk(near), near[2]]
    slab_0 = lax.dynamic_slice_in_dim(panel_0, y * rows, rows, 0)
    sent_0 = along_x(slab_0, 0, (1, -1, 2))
    partial = [partial_of(panel_0)]

    chunks, partial[0], sent_1 = lax.optimization_barrier((chunks, partial[0], sent_1))
    across = from_root(
        jnp.where(first, slab_1, slab_0), lambda x, c, z, y: (x, 1 - c, z, y)
    )
    partial.append(partial_of(placed_by_owner(chunks, y, 1).reshape(panel_0.shape)))

    partial[1], sent_0[:2] = lax.optimization_barrier((partial[1], sent_0[:2]))
    pair = lax.optimization_barrier(pair_sum(partial))
    sent = [*sent_1, *sent_0, across]
    home = row == z
    slab = jnp.where(first, slab_0, slab_1)
    factor_slab = sum(sent, jnp.where(home, slab, jnp.zeros((), BF16)))
    product = sum_over_x(pair)
    col_keep = lax.dynamic_index_in_dim(keep_of(col * rows, rows), core, 0)
    offdiag = lax.optimization_barrier((-(product * col_keep)).astype(BF16))

    term = -jnp.dot(offdiag, factor_slab, preferred_element_type=F32)
    correction = own_slab_of_both(summed_over_col(term.astype(BF16)))
    return (
        own_slab_of_both(offdiag).transpose(0, 2, 1),
        diag_inv + correction.astype(F32).transpose(0, 2, 1),
    )


def solution(mesh):
    torus = Mesh(mesh.devices.reshape(XS, CORES, ZS, YS), ALL)
    return jax.shard_map(
        body,
        mesh=torus,
        in_specs=(P(), P(None, ALL, None), P(), P(COL, ROW), P(None, None, ROW)),
        out_specs=(P(None, COL, ROW), P(None, None, ROW)),
        check_vma=False,
    )
```

```python
import jax
import jax.numpy as jnp
from jax import lax
from jax.sharding import Mesh
from jax.sharding import PartitionSpec as P

NSEL = 40
XS, CORES, ZS, YS = 4, 2, 8, 4
ROW = ("x", "core")
COL = ("z", "y")
ALL = ("x", "core", "z", "y")
F32 = jnp.float32
BF16 = jnp.bfloat16


def shift(array, axis, size, by):
    return lax.ppermute(array, axis, [(i, (i + by) % size) for i in range(size)])


def direct_ring(array, axis, size):
    return [array] + [shift(array, axis, size, d if d <= size // 2 else d - size) for d in range(1, size)]


def relay_ring(array, axis, size, halved):
    got = [array] + [None] * (size - 1)
    right = left = array
    for step in range(1, size // 2):
        right = shift(right, axis, size, 1)
        left = shift(left, axis, size, -1)
        got[step], got[size - step] = right, left
    if halved:
        half = array.shape[0] // 2
        got[size // 2] = jnp.concatenate(
            [shift(right[:half], axis, size, 1), shift(left[half:], axis, size, -1)], axis=0
        )
    else:
        got[size // 2] = shift(right, axis, size, 1)
    return got


def placed_by_owner(got, own, axis):
    size, width = len(got), got[0].shape[axis]
    dims = list(got[0].shape)
    dims[axis] *= size
    whole = jnp.zeros(dims, got[0].dtype)
    for d, chunk in enumerate(got):
        whole = lax.dynamic_update_slice_in_dim(whole, chunk, (own - d) % size * width, axis)
    return whole


def panel_y_then_z(piece):
    part = placed_by_owner(direct_ring(piece, "y", YS), lax.axis_index("y"), 0)
    return lax.all_gather(part, "z", axis=0, tiled=True)


def near_z_then_y(piece):
    part = placed_by_owner(relay_ring(piece[None], "z", ZS, False), lax.axis_index("z"), 0)[:, None]
    return [part, shift(part, "y", YS, 1), shift(part, "y", YS, -1)]


def far_chunk(near):
    half = near[0].shape[0] // 2
    right = shift(near[1][:half], "y", YS, 1)
    return jnp.concatenate([right, shift(near[2][half:], "y", YS, -1)], axis=0)


def device(x, core, z, y):
    return ((x * CORES + core) * ZS + z) * YS + y


def root_of(z):
    return z // CORES, z % CORES


def from_root(array, target):
    pairs = []
    for z in range(ZS):
        for y in range(YS):
            x, core = root_of(z)
            pairs.append((device(x, core, z, y), device(*target(x, core, z, y))))
    return lax.ppermute(array, ALL, pairs)


def to_ring(tiles, core):
    return [
        from_root(tiles[by], lambda x, c, z, y: ((x + by) % XS, core, z, y)) for by in (1, 2, 3)
    ]


def pair_sum(partial):
    first = lax.axis_index("core") == 0
    given = lax.ppermute(jnp.where(first, partial[1], partial[0]), "core", [(0, 1), (1, 0)])
    pair = jnp.where(first, partial[0], partial[1]).astype(F32) + given.astype(F32)
    return pair.astype(BF16)


def sum_over_x(pair):
    x = lax.axis_index("x")
    pair = pair.reshape(XS, -1, pair.shape[1])
    tile = lambda k: lax.dynamic_index_in_dim(pair, (x + k) % XS, 0, keepdims=False)
    opposite = shift(tile(2), "x", XS, 2)
    near = shift(tile(1), "x", XS, 1).astype(F32) + shift(tile(3), "x", XS, -1).astype(F32)
    return (tile(0).astype(F32) + opposite.astype(F32)) + near


def exchanged(array, axis, size, by):
    return lax.ppermute(array, axis, [(i, i ^ by) for i in range(size)])


def summed_over_col(array):
    y = lax.axis_index("y")
    quarters = array.reshape(YS, -1, array.shape[1])
    own = lambda k: lax.dynamic_index_in_dim(quarters, y ^ k, 0, keepdims=False)
    part = own(0).astype(F32)
    for k in range(1, YS):
        part = part + exchanged(own(k), "y", YS, k).astype(F32)
    part = lax.optimization_barrier(part.astype(BF16))
    copies = jnp.broadcast_to(part[None], (ZS, *part.shape))
    part = lax.all_to_all(copies, "z", split_axis=0, concat_axis=0, tiled=True)
    part = lax.optimization_barrier(part.astype(F32).sum(axis=0).astype(BF16))
    whole = jnp.zeros(quarters.shape, BF16)
    for k in range(YS):
        got = part if k == 0 else exchanged(part, "y", YS, k)
        whole = lax.dynamic_update_slice_in_dim(whole, got[None], y ^ k, 0)
    return whole.reshape(array.shape)


def own_slab_of_both(array):
    core = lax.axis_index("core")
    slabs = array.reshape(CORES, -1, array.shape[1])
    kept = lax.dynamic_index_in_dim(slabs, core, 0, keepdims=False)
    given = lax.dynamic_index_in_dim(slabs, 1 - core, 0, keepdims=False)
    got = lax.ppermute(given, "core", [(0, 1), (1, 0)])
    return jnp.stack([jnp.where(core == 0, kept, got), jnp.where(core == 0, got, kept)])


def body(listing, pieces, factor_inv, inverse_block, diag_inv):
    piece_rows, width = pieces.shape[1:]
    row = lax.axis_index(ROW)
    col = lax.axis_index(COL)
    core, z, y = lax.axis_index("core"), lax.axis_index("z"), lax.axis_index("y")
    chosen = listing[:, :NSEL]

    def keep_of(first, count):
        labels = (first + jnp.arange(count, dtype=jnp.int32)) // width
        return jnp.any(chosen[:, :, None] == labels[None, None, :], axis=1).astype(F32)

    own_keep = keep_of((row * ZS * YS + col) * piece_rows, piece_rows)
    normed = jnp.einsum("srk,skj->srj", pieces, factor_inv, preferred_element_type=F32)
    normed = (normed * own_keep[:, :, None]).astype(BF16)
    rows = inverse_block.shape[0]

    def partial_of(panel):
        return jnp.dot(inverse_block, panel, preferred_element_type=F32).astype(BF16)

    first = core == 0
    near = near_z_then_y(normed[1])

    deep = rows // (piece_rows * YS)
    of_slab = lambda part, lane: lax.dynamic_slice_in_dim(part, lane * deep, deep, 0)
    far_part = from_root(
        of_slab(near[0], (y + 2) % YS), lambda x, c, z, y: (x, c, z, (y + 2) % YS)
    )
    slab_parts = [of_slab(near[0], y), of_slab(near[1], y), far_part, of_slab(near[2], y)]
    slab_1 = placed_by_owner(slab_parts, y, 1).reshape(rows, width)
    x = lax.axis_index("x")
    share = rows // XS
    chip = lambda by: (z // CORES + by) % XS
    tiles_1 = [lax.dynamic_slice_in_dim(slab_1, chip(by) * share, share, 0) for by in range(XS)]
    panel_0 = panel_y_then_z(normed[0])
    panel_0, near, tiles_1 = lax.optimization_barrier((panel_0, near, tiles_1))
    chunks = [near[0], near[1], far_chunk(near), near[2]]
    tiles_0 = [
        lax.dynamic_slice_in_dim(panel_0, y * rows + chip(by) * share, share, 0) for by in range(XS)
    ]
    sent_1, sent_0 = to_ring(tiles_1, 1), to_ring(tiles_0, 0)
    across = from_root(
        jnp.where(first, tiles_1[0], tiles_0[0]), lambda x, c, z, y: (x, 1 - c, z, y)
    )
    partial = [partial_of(panel_0)]

    chunks, partial[0], sent_1 = lax.optimization_barrier((chunks, partial[0], sent_1))
    partial.append(partial_of(placed_by_owner(chunks, y, 1).reshape(panel_0.shape)))

    sent = [*sent_1, *sent_0, across]
    pair, sent = lax.optimization_barrier((pair_sum(partial), sent))
    product = sum_over_x(pair)
    own_tile = jnp.where(first, tiles_0[0], tiles_1[0])
    factor_tile = sum(sent, jnp.where(row == z, own_tile, jnp.zeros((), BF16)))
    tile_keep = lax.dynamic_index_in_dim(keep_of(col * rows + x * share, share), core, 0)
    offdiag_tile = lax.optimization_barrier((-(product * tile_keep.T)).astype(BF16))

    term = -jnp.einsum("pk,pj->kj", offdiag_tile, factor_tile, preferred_element_type=F32)
    term = sum_over_x(lax.optimization_barrier(term.astype(BF16)))
    correction = own_slab_of_both(summed_over_col(term.astype(BF16)))

    sent_to = lambda by: lax.dynamic_slice_in_dim(
        offdiag_tile, (x + by) % XS * (width // XS), width // XS, 1
    )
    got = [sent_to(0)] + [shift(sent_to(by), "x", XS, by) for by in range(1, XS)]
    offdiag = placed_by_owner(got, x, 0).T
    return (
        own_slab_of_both(offdiag).transpose(0, 2, 1),
        diag_inv + correction.astype(F32).transpose(0, 2, 1),
    )


def solution(mesh):
    torus = Mesh(mesh.devices.reshape(XS, CORES, ZS, YS), ALL)
    return jax.shard_map(
        body,
        mesh=torus,
        in_specs=(P(), P(None, ALL, None), P(), P(COL, ROW), P(None, None, ROW)),
        out_specs=(P(None, COL, ROW), P(None, None, ROW)),
        check_vma=False,
    )
```

```python
import jax
import jax.numpy as jnp
from jax import lax
from jax.sharding import Mesh
from jax.sharding import PartitionSpec as P

NSEL = 40
XS, CORES, ZS, YS = 4, 2, 8, 4
ROW = ("x", "core")
COL = ("z", "y")
ALL = ("x", "core", "z", "y")
F32 = jnp.float32
BF16 = jnp.bfloat16


def shift(array, axis, size, by):
    return lax.ppermute(array, axis, [(i, (i + by) % size) for i in range(size)])


def direct_ring(array, axis, size):
    return [array] + [shift(array, axis, size, d if d <= size // 2 else d - size) for d in range(1, size)]


def relay_ring(array, axis, size, halved):
    got = [array] + [None] * (size - 1)
    right = left = array
    for step in range(1, size // 2):
        right = shift(right, axis, size, 1)
        left = shift(left, axis, size, -1)
        got[step], got[size - step] = right, left
    if halved:
        half = array.shape[0] // 2
        got[size // 2] = jnp.concatenate(
            [shift(right[:half], axis, size, 1), shift(left[half:], axis, size, -1)], axis=0
        )
    else:
        got[size // 2] = shift(right, axis, size, 1)
    return got


def placed_by_owner(got, own, axis, order=None):
    size, width = len(got), got[0].shape[axis]
    dims = list(got[0].shape)
    dims[axis] *= size
    whole = jnp.zeros(dims, got[0].dtype)
    for d in order or range(size):
        whole = lax.dynamic_update_slice_in_dim(whole, got[d], (own - d) % size * width, axis)
    return whole


def panel_y_then_z(piece):
    part = placed_by_owner(direct_ring(piece, "y", YS), lax.axis_index("y"), 0)
    return lax.all_gather(part, "z", axis=0, tiled=True)


def near_z_then_y(piece):
    part = placed_by_owner(relay_ring(piece[None], "z", ZS, False), lax.axis_index("z"), 0)[:, None]
    return [part, shift(part, "y", YS, 1), shift(part, "y", YS, -1)]


def far_chunk(near):
    half = near[0].shape[0] // 2
    right = shift(near[1][:half], "y", YS, 1)
    return jnp.concatenate([right, shift(near[2][half:], "y", YS, -1)], axis=0)


def device(x, core, z, y):
    return ((x * CORES + core) * ZS + z) * YS + y


def root_of(z):
    return z // CORES, z % CORES


def from_root(array, target):
    pairs = []
    for z in range(ZS):
        for y in range(YS):
            x, core = root_of(z)
            pairs.append((device(x, core, z, y), device(*target(x, core, z, y))))
    return lax.ppermute(array, ALL, pairs)


def to_ring(tiles, core):
    return [
        from_root(tiles[by], lambda x, c, z, y: ((x + by) % XS, core, z, y)) for by in (1, 2, 3)
    ]


def pair_sum(partial):
    first = lax.axis_index("core") == 0
    given = lax.ppermute(jnp.where(first, partial[1], partial[0]), "core", [(0, 1), (1, 0)])
    pair = jnp.where(first, partial[0], partial[1]).astype(F32) + given.astype(F32)
    return pair.astype(BF16)


def sum_over_x(pair):
    x = lax.axis_index("x")
    pair = pair.reshape(XS, -1, pair.shape[1])
    tile = lambda k: lax.dynamic_index_in_dim(pair, (x + k) % XS, 0, keepdims=False)
    opposite = shift(tile(2), "x", XS, 2)
    near = shift(tile(1), "x", XS, 1).astype(F32) + shift(tile(3), "x", XS, -1).astype(F32)
    return (tile(0).astype(F32) + opposite.astype(F32)) + near


def exchanged(array, axis, size, by):
    return lax.ppermute(array, axis, [(i, i ^ by) for i in range(size)])


def summed_over_col(array):
    y = lax.axis_index("y")
    quarters = array.reshape(YS, -1, array.shape[1])
    own = lambda k: lax.dynamic_index_in_dim(quarters, y ^ k, 0, keepdims=False)
    part = own(0).astype(F32)
    for k in range(1, YS):
        part = part + exchanged(own(k), "y", YS, k).astype(F32)
    part = lax.optimization_barrier(part.astype(BF16))
    copies = jnp.broadcast_to(part[None], (ZS, *part.shape))
    part = lax.all_to_all(copies, "z", split_axis=0, concat_axis=0, tiled=True)
    part = lax.optimization_barrier(part.astype(F32).sum(axis=0).astype(BF16))
    whole = jnp.zeros(quarters.shape, BF16)
    for k in range(YS):
        got = part if k == 0 else exchanged(part, "y", YS, k)
        whole = lax.dynamic_update_slice_in_dim(whole, got[None], y ^ k, 0)
    return whole.reshape(array.shape)


def own_slab_of_both(array):
    core = lax.axis_index("core")
    slabs = array.reshape(CORES, -1, array.shape[1])
    kept = lax.dynamic_index_in_dim(slabs, core, 0, keepdims=False)
    given = lax.dynamic_index_in_dim(slabs, 1 - core, 0, keepdims=False)
    got = lax.ppermute(given, "core", [(0, 1), (1, 0)])
    return jnp.stack([jnp.where(core == 0, kept, got), jnp.where(core == 0, got, kept)])


def body(listing, pieces, factor_inv, inverse_block, diag_inv):
    piece_rows, width = pieces.shape[1:]
    row = lax.axis_index(ROW)
    col = lax.axis_index(COL)
    core, z, y = lax.axis_index("core"), lax.axis_index("z"), lax.axis_index("y")
    chosen = listing[:, :NSEL]

    def keep_of(first, count):
        labels = (first + jnp.arange(count, dtype=jnp.int32)) // width
        return jnp.any(chosen[:, :, None] == labels[None, None, :], axis=1).astype(F32)

    own_keep = keep_of((row * ZS * YS + col) * piece_rows, piece_rows)
    normed = jnp.einsum("srk,skj->srj", pieces, factor_inv, preferred_element_type=F32)
    normed = (normed * own_keep[:, :, None]).astype(BF16)
    rows = inverse_block.shape[0]

    def partial_of(panel):
        return jnp.dot(inverse_block, panel, preferred_element_type=F32).astype(BF16)

    first = core == 0
    near = near_z_then_y(normed[1])

    deep = rows // (piece_rows * YS)
    of_slab = lambda part, lane: lax.dynamic_slice_in_dim(part, lane * deep, deep, 0)
    far_part = from_root(
        of_slab(near[0], (y + 2) % YS), lambda x, c, z, y: (x, c, z, (y + 2) % YS)
    )
    slab_parts = [of_slab(near[0], y), of_slab(near[1], y), far_part, of_slab(near[2], y)]
    slab_1 = placed_by_owner(slab_parts, y, 1).reshape(rows, width)
    x = lax.axis_index("x")
    share = rows // XS
    chip = lambda by: (z // CORES + by) % XS
    tiles_1 = [lax.dynamic_slice_in_dim(slab_1, chip(by) * share, share, 0) for by in range(XS)]
    panel_0 = panel_y_then_z(normed[0])
    panel_0, tiles_1 = lax.optimization_barrier((panel_0, tiles_1))
    far = far_chunk(near)
    tiles_0 = [
        lax.dynamic_slice_in_dim(panel_0, y * rows + chip(by) * share, share, 0) for by in range(XS)
    ]
    sent_1, sent_0 = to_ring(tiles_1, 1), to_ring(tiles_0, 0)
    across = from_root(
        jnp.where(first, tiles_1[0], tiles_0[0]), lambda x, c, z, y: (x, 1 - c, z, y)
    )
    partial = [partial_of(panel_0)]

    near, partial[0], sent_1 = lax.optimization_barrier((near, partial[0], sent_1))
    panel_1 = placed_by_owner([near[0], near[1], far, near[2]], y, 1, (0, 1, 3, 2))
    partial.append(partial_of(panel_1.reshape(panel_0.shape)))

    sent = [*sent_1, *sent_0, across]
    pair, sent = lax.optimization_barrier((pair_sum(partial), sent))
    product = sum_over_x(pair)
    own_tile = jnp.where(first, tiles_0[0], tiles_1[0])
    factor_tile = sum(sent, jnp.where(row == z, own_tile, jnp.zeros((), BF16)))
    tile_keep = lax.dynamic_index_in_dim(keep_of(col * rows + x * share, share), core, 0)
    offdiag_tile = lax.optimization_barrier((-(product * tile_keep.T)).astype(BF16))

    term = -jnp.einsum("pk,pj->kj", offdiag_tile, factor_tile, preferred_element_type=F32)
    term = sum_over_x(lax.optimization_barrier(term.astype(BF16)))
    correction = own_slab_of_both(summed_over_col(term.astype(BF16)))

    sent_to = lambda by: lax.dynamic_slice_in_dim(
        offdiag_tile, (x + by) % XS * (width // XS), width // XS, 1
    )
    got = [sent_to(0)] + [shift(sent_to(by), "x", XS, by) for by in range(1, XS)]
    offdiag = placed_by_owner(got, x, 0).T
    return (
        own_slab_of_both(offdiag).transpose(0, 2, 1),
        diag_inv + correction.astype(F32).transpose(0, 2, 1),
    )


def solution(mesh):
    torus = Mesh(mesh.devices.reshape(XS, CORES, ZS, YS), ALL)
    return jax.shard_map(
        body,
        mesh=torus,
        in_specs=(P(), P(None, ALL, None), P(), P(COL, ROW), P(None, None, ROW)),
        out_specs=(P(None, COL, ROW), P(None, None, ROW)),
        check_vma=False,
    )
```

```python
import jax
import jax.numpy as jnp
from jax import lax
from jax.sharding import Mesh
from jax.sharding import PartitionSpec as P

NSEL = 40
XS, CORES, ZS, YS = 4, 2, 8, 4
ROW = ("x", "core")
COL = ("z", "y")
ALL = ("x", "core", "z", "y")
F32 = jnp.float32
BF16 = jnp.bfloat16


def shift(array, axis, size, by):
    return lax.ppermute(array, axis, [(i, (i + by) % size) for i in range(size)])


def direct_ring(array, axis, size):
    return [array] + [shift(array, axis, size, d if d <= size // 2 else d - size) for d in range(1, size)]


def relay_ring(array, axis, size, halved):
    got = [array] + [None] * (size - 1)
    right = left = array
    for step in range(1, size // 2):
        right = shift(right, axis, size, 1)
        left = shift(left, axis, size, -1)
        got[step], got[size - step] = right, left
    if halved:
        half = array.shape[0] // 2
        got[size // 2] = jnp.concatenate(
            [shift(right[:half], axis, size, 1), shift(left[half:], axis, size, -1)], axis=0
        )
    else:
        got[size // 2] = shift(right, axis, size, 1)
    return got


def placed_by_owner(got, own, axis):
    size, width = len(got), got[0].shape[axis]
    dims = list(got[0].shape)
    dims[axis] *= size
    whole = jnp.zeros(dims, got[0].dtype)
    for d, chunk in enumerate(got):
        whole = lax.dynamic_update_slice_in_dim(whole, chunk, (own - d) % size * width, axis)
    return whole


def panel_y_then_z(piece):
    part = placed_by_owner(direct_ring(piece, "y", YS), lax.axis_index("y"), 0)
    return lax.all_gather(part, "z", axis=0, tiled=True)


def near_z_then_y(piece):
    part = placed_by_owner(relay_ring(piece[None], "z", ZS, False), lax.axis_index("z"), 0)[:, None]
    return [part, shift(part, "y", YS, 1), shift(part, "y", YS, -1)]


def far_chunk(near):
    half = near[0].shape[0] // 2
    right = shift(near[1][:half], "y", YS, 1)
    return jnp.concatenate([right, shift(near[2][half:], "y", YS, -1)], axis=0)


def device(x, core, z, y):
    return ((x * CORES + core) * ZS + z) * YS + y


def root_of(z):
    return z // CORES, z % CORES


def from_root(array, target):
    pairs = []
    for z in range(ZS):
        for y in range(YS):
            x, core = root_of(z)
            pairs.append((device(x, core, z, y), device(*target(x, core, z, y))))
    return lax.ppermute(array, ALL, pairs)


def along_x(slab, core, shifts):
    return sum(from_root(slab, lambda x, c, z, y: ((x + by) % XS, core, z, y)) for by in shifts)


def pair_sum(partial):
    first = lax.axis_index("core") == 0
    given = lax.ppermute(jnp.where(first, partial[1], partial[0]), "core", [(0, 1), (1, 0)])
    pair = jnp.where(first, partial[0], partial[1]).astype(F32) + given.astype(F32)
    return pair.astype(BF16)


def sum_over_x(pair):
    x = lax.axis_index("x")
    pair = pair.reshape(XS, -1, pair.shape[1])
    tile = lambda k: lax.dynamic_index_in_dim(pair, (x + k) % XS, 0, keepdims=False)
    opposite = shift(tile(2), "x", XS, 2)
    near = shift(tile(1), "x", XS, 1).astype(F32) + shift(tile(3), "x", XS, -1).astype(F32)
    return (tile(0).astype(F32) + opposite.astype(F32)) + near


def exchanged(array, axis, size, by):
    return lax.ppermute(array, axis, [(i, i ^ by) for i in range(size)])


def summed_over_col(array):
    y = lax.axis_index("y")
    quarters = array.reshape(YS, -1, array.shape[1])
    own = lambda k: lax.dynamic_index_in_dim(quarters, y ^ k, 0, keepdims=False)
    part = own(0).astype(F32)
    for k in range(1, YS):
        part = part + exchanged(own(k), "y", YS, k).astype(F32)
    part = lax.optimization_barrier(part.astype(BF16))
    copies = jnp.broadcast_to(part[None], (ZS, *part.shape))
    part = lax.all_to_all(copies, "z", split_axis=0, concat_axis=0, tiled=True)
    part = lax.optimization_barrier(part.astype(F32).sum(axis=0).astype(BF16))
    whole = jnp.zeros(quarters.shape, BF16)
    for k in range(YS):
        got = part if k == 0 else exchanged(part, "y", YS, k)
        whole = lax.dynamic_update_slice_in_dim(whole, got[None], y ^ k, 0)
    return whole.reshape(array.shape)


def own_slab_of_both(array):
    core = lax.axis_index("core")
    slabs = array.reshape(CORES, -1, array.shape[1])
    kept = lax.dynamic_index_in_dim(slabs, core, 0, keepdims=False)
    given = lax.dynamic_index_in_dim(slabs, 1 - core, 0, keepdims=False)
    got = lax.ppermute(given, "core", [(0, 1), (1, 0)])
    return jnp.stack([jnp.where(core == 0, kept, got), jnp.where(core == 0, got, kept)])


def body(listing, pieces, factor_inv, inverse_block, diag_inv):
    piece_rows, width = pieces.shape[1:]
    row = lax.axis_index(ROW)
    col = lax.axis_index(COL)
    core, z, y = lax.axis_index("core"), lax.axis_index("z"), lax.axis_index("y")
    chosen = listing[:, :NSEL]

    def keep_of(first, count):
        labels = (first + jnp.arange(count, dtype=jnp.int32)) // width
        return jnp.any(chosen[:, :, None] == labels[None, None, :], axis=1).astype(F32)

    own_keep = keep_of((row * ZS * YS + col) * piece_rows, piece_rows)
    normed = jnp.einsum("srk,skj->srj", pieces, factor_inv, preferred_element_type=F32)
    normed = (normed * own_keep[:, :, None]).astype(BF16)
    rows = inverse_block.shape[0]

    def partial_of(panel):
        return jnp.einsum("qj,pq->jp", panel, inverse_block, preferred_element_type=F32).astype(BF16)

    first = core == 0
    near = near_z_then_y(normed[1])

    deep = rows // (piece_rows * YS)
    of_slab = lambda part, lane: lax.dynamic_slice_in_dim(part, lane * deep, deep, 0)
    far_part = from_root(
        of_slab(near[0], (y + 2) % YS), lambda x, c, z, y: (x, c, z, (y + 2) % YS)
    )
    slab_parts = [of_slab(near[0], y), of_slab(near[1], y), far_part, of_slab(near[2], y)]
    slab_1 = placed_by_owner(slab_parts, y, 1).reshape(rows, width)
    sent_1 = along_x(slab_1, 1, (1, -1, -2))

    panel_0 = panel_y_then_z(normed[0])
    panel_0, near = lax.optimization_barrier((panel_0, near))
    chunks = [near[0], near[1], far_chunk(near), near[2]]
    slab_0 = lax.dynamic_slice_in_dim(panel_0, y * rows, rows, 0)
    sent_0 = along_x(slab_0, 0, (1, -1, 2))
    partial = [partial_of(panel_0)]

    chunks, partial[0] = lax.optimization_barrier((chunks, partial[0]))
    across = from_root(
        jnp.where(first, slab_1, slab_0), lambda x, c, z, y: (x, 1 - c, z, y)
    )
    partial.append(partial_of(placed_by_owner(chunks, y, 1).reshape(panel_0.shape)))

    home = row == z
    factor_slab = jnp.where(home, jnp.where(first, slab_0, slab_1), sent_0 + sent_1 + across)
    pair, factor_slab = lax.optimization_barrier((pair_sum(partial), factor_slab))
    product = sum_over_x(pair)
    col_keep = lax.dynamic_index_in_dim(keep_of(col * rows, rows), core, 0)
    offdiag = lax.optimization_barrier((-(product * col_keep)).astype(BF16))

    term = -jnp.dot(offdiag, factor_slab, preferred_element_type=F32)
    correction = own_slab_of_both(summed_over_col(term.astype(BF16)))
    return (
        own_slab_of_both(offdiag).transpose(0, 2, 1),
        diag_inv + correction.astype(F32).transpose(0, 2, 1),
    )


def solution(mesh):
    torus = Mesh(mesh.devices.reshape(XS, CORES, ZS, YS), ALL)
    return jax.shard_map(
        body,
        mesh=torus,
        in_specs=(P(), P(None, ALL, None), P(), P(COL, ROW), P(None, None, ROW)),
        out_specs=(P(None, COL, ROW), P(None, None, ROW)),
        check_vma=False,
    )
```

```python
import jax
import jax.numpy as jnp
from jax import lax
from jax.experimental import pallas as pl
from jax.experimental.pallas import tpu as pltpu
from jax.sharding import Mesh
from jax.sharding import PartitionSpec as P

NSEL = 40
XS, CORES, ZS, YS = 4, 2, 8, 4
ROW = ("x", "core")
COL = ("z", "y")
ALL = ("x", "core", "z", "y")
F32 = jnp.float32
BF16 = jnp.bfloat16


def shift(array, axis, size, by):
    return lax.ppermute(array, axis, [(i, (i + by) % size) for i in range(size)])


def direct_ring(array, axis, size):
    return [array] + [shift(array, axis, size, d if d <= size // 2 else d - size) for d in range(1, size)]


def relay_ring(array, axis, size, halved):
    got = [array] + [None] * (size - 1)
    right = left = array
    for step in range(1, size // 2):
        right = shift(right, axis, size, 1)
        left = shift(left, axis, size, -1)
        got[step], got[size - step] = right, left
    if halved:
        half = array.shape[0] // 2
        got[size // 2] = jnp.concatenate(
            [shift(right[:half], axis, size, 1), shift(left[half:], axis, size, -1)], axis=0
        )
    else:
        got[size // 2] = shift(right, axis, size, 1)
    return got


def placed_by_owner(got, own, axis):
    size, width = len(got), got[0].shape[axis]
    dims = list(got[0].shape)
    dims[axis] *= size
    whole = jnp.zeros(dims, got[0].dtype)
    for d, chunk in enumerate(got):
        whole = lax.dynamic_update_slice_in_dim(whole, chunk, (own - d) % size * width, axis)
    return whole


def panel_y_then_z(piece):
    part = placed_by_owner(direct_ring(piece, "y", YS), lax.axis_index("y"), 0)
    return lax.all_gather(part, "z", axis=0, tiled=True)


def near_z_then_y(piece):
    part = placed_by_owner(relay_ring(piece[None], "z", ZS, False), lax.axis_index("z"), 0)[:, None]
    return [part, shift(part, "y", YS, 1), shift(part, "y", YS, -1)]


def far_chunk(near):
    half = near[0].shape[0] // 2
    right = shift(near[1][:half], "y", YS, 1)
    return jnp.concatenate([right, shift(near[2][half:], "y", YS, -1)], axis=0)


def device(x, core, z, y):
    return ((x * CORES + core) * ZS + z) * YS + y


def root_of(z):
    return z // CORES, z % CORES


def from_root(array, target):
    pairs = []
    for z in range(ZS):
        for y in range(YS):
            x, core = root_of(z)
            pairs.append((device(x, core, z, y), device(*target(x, core, z, y))))
    return lax.ppermute(array, ALL, pairs)


def along_x(slab, core, shifts):
    return sum(from_root(slab, lambda x, c, z, y: ((x + by) % XS, core, z, y)) for by in shifts)


def pair_sum(partial):
    first = lax.axis_index("core") == 0
    given = lax.ppermute(jnp.where(first, partial[1], partial[0]), "core", [(0, 1), (1, 0)])
    pair = jnp.where(first, partial[0], partial[1]).astype(F32) + given.astype(F32)
    return pair.astype(BF16)


def sum_over_x(pair):
    x = lax.axis_index("x")
    pair = pair.reshape(XS, -1, pair.shape[1])
    tile = lambda k: lax.dynamic_index_in_dim(pair, (x + k) % XS, 0, keepdims=False)
    opposite = shift(tile(2), "x", XS, 2)
    near = shift(tile(1), "x", XS, 1).astype(F32) + shift(tile(3), "x", XS, -1).astype(F32)
    return (tile(0).astype(F32) + opposite.astype(F32)) + near


def exchanged(array, axis, size, by):
    return lax.ppermute(array, axis, [(i, i ^ by) for i in range(size)])


def summed_over_col(array):
    y = lax.axis_index("y")
    quarters = array.reshape(YS, -1, array.shape[1])
    own = lambda k: lax.dynamic_index_in_dim(quarters, y ^ k, 0, keepdims=False)
    part = own(0).astype(F32)
    for k in range(1, YS):
        part = part + exchanged(own(k), "y", YS, k).astype(F32)
    part = lax.optimization_barrier(part.astype(BF16))
    copies = jnp.broadcast_to(part[None], (ZS, *part.shape))
    part = lax.all_to_all(copies, "z", split_axis=0, concat_axis=0, tiled=True)
    part = lax.optimization_barrier(part.astype(F32).sum(axis=0).astype(BF16))
    whole = jnp.zeros(quarters.shape, BF16)
    for k in range(YS):
        got = part if k == 0 else exchanged(part, "y", YS, k)
        whole = lax.dynamic_update_slice_in_dim(whole, got[None], y ^ k, 0)
    return whole.reshape(array.shape)


def own_slab_of_both(array):
    core = lax.axis_index("core")
    slabs = array.reshape(CORES, -1, array.shape[1])
    kept = lax.dynamic_index_in_dim(slabs, core, 0, keepdims=False)
    given = lax.dynamic_index_in_dim(slabs, 1 - core, 0, keepdims=False)
    got = lax.ppermute(given, "core", [(0, 1), (1, 0)])
    return jnp.stack([jnp.where(core == 0, kept, got), jnp.where(core == 0, got, kept)])


def streamed_product(block, panel, depth):
    rows, inner = block.shape
    width = panel.shape[1]

    def step(block_ref, panel_ref, out_ref, total):
        k = pl.program_id(0)
        part = jnp.dot(block_ref[...], panel_ref[...], preferred_element_type=F32)

        @pl.when(k == 0)
        def _():
            total[...] = part

        @pl.when(k > 0)
        def _():
            total[...] += part

        @pl.when(k == pl.num_programs(0) - 1)
        def _():
            out_ref[...] = total[...].T.astype(BF16)

    return pl.pallas_call(
        step,
        grid=(inner // depth,),
        in_specs=[
            pl.BlockSpec((rows, depth), lambda k: (0, k)),
            pl.BlockSpec((depth, width), lambda k: (k, 0)),
        ],
        out_specs=pl.BlockSpec((width, rows), lambda k: (0, 0)),
        out_shape=jax.ShapeDtypeStruct((width, rows), BF16),
        scratch_shapes=[pltpu.VMEM((rows, width), F32)],
        compiler_params=pltpu.CompilerParams(
            dimension_semantics=("arbitrary",), vmem_limit_bytes=32 << 20
        ),
        cost_estimate=pl.CostEstimate(
            flops=2 * rows * inner * width,
            transcendentals=0,
            bytes_accessed=2 * (rows * inner + inner * width + rows * width),
        ),
    )(block, panel)


def body(listing, pieces, factor_inv, inverse_block, diag_inv):
    piece_rows, width = pieces.shape[1:]
    row = lax.axis_index(ROW)
    col = lax.axis_index(COL)
    core, z, y = lax.axis_index("core"), lax.axis_index("z"), lax.axis_index("y")
    chosen = listing[:, :NSEL]

    def keep_of(first, count):
        labels = (first + jnp.arange(count, dtype=jnp.int32)) // width
        return jnp.any(chosen[:, :, None] == labels[None, None, :], axis=1).astype(F32)

    first_row = (row * ZS * YS + col) * piece_rows
    ends = jnp.stack([first_row, first_row + piece_rows - 1]) // width
    kept = jnp.any(chosen[:, :, None] == ends[None, None, :], axis=1).astype(F32)
    in_last = first_row + jnp.arange(piece_rows, dtype=jnp.int32) >= ends[1] * width
    own_keep = jnp.where(in_last[None, :], kept[:, 1:], kept[:, :1])
    normed = jnp.einsum("srk,skj->srj", pieces, factor_inv, preferred_element_type=F32)
    normed = (normed * own_keep[:, :, None]).astype(BF16)
    rows = inverse_block.shape[0]

    def partial_of(panel):
        return jnp.einsum("qj,pq->jp", panel, inverse_block, preferred_element_type=F32).astype(BF16)

    first = core == 0
    near = near_z_then_y(normed[1])

    deep = rows // (piece_rows * YS)
    of_slab = lambda part, lane: lax.dynamic_slice_in_dim(part, lane * deep, deep, 0)
    far_part = from_root(
        of_slab(near[0], (y + 2) % YS), lambda x, c, z, y: (x, c, z, (y + 2) % YS)
    )
    slab_parts = [of_slab(near[0], y), of_slab(near[1], y), far_part, of_slab(near[2], y)]
    slab_1 = placed_by_owner(slab_parts, y, 1).reshape(rows, width)
    sent_1 = along_x(slab_1, 1, (1, -1, -2))

    panel_0 = panel_y_then_z(normed[0])
    panel_0, near = lax.optimization_barrier((panel_0, near))
    chunks = [near[0], near[1], far_chunk(near), near[2]]
    slab_0 = lax.dynamic_slice_in_dim(panel_0, y * rows, rows, 0)
    sent_0 = along_x(slab_0, 0, (1, -1, 2))
    partial = [streamed_product(inverse_block, panel_0, 512)]

    chunks, partial[0] = lax.optimization_barrier((chunks, partial[0]))
    across = from_root(
        jnp.where(first, slab_1, slab_0), lambda x, c, z, y: (x, 1 - c, z, y)
    )
    partial.append(partial_of(placed_by_owner(chunks, y, 1).reshape(panel_0.shape)))

    home = row == z
    factor_slab = jnp.where(home, jnp.where(first, slab_0, slab_1), sent_0 + sent_1 + across)
    pair, factor_slab = lax.optimization_barrier((pair_sum(partial), factor_slab))
    product = sum_over_x(pair)
    col_keep = lax.dynamic_index_in_dim(keep_of(col * rows, rows), core, 0)
    offdiag = lax.optimization_barrier((-(product * col_keep)).astype(BF16))

    term = -jnp.dot(offdiag, factor_slab, preferred_element_type=F32)
    correction = own_slab_of_both(summed_over_col(term.astype(BF16)))
    return (
        own_slab_of_both(offdiag).transpose(0, 2, 1),
        diag_inv + correction.astype(F32).transpose(0, 2, 1),
    )


def solution(mesh):
    torus = Mesh(mesh.devices.reshape(XS, CORES, ZS, YS), ALL)
    return jax.shard_map(
        body,
        mesh=torus,
        in_specs=(P(), P(None, ALL, None), P(), P(COL, ROW), P(None, None, ROW)),
        out_specs=(P(None, COL, ROW), P(None, None, ROW)),
        check_vma=False,
    )
```

```python
import jax
import jax.numpy as jnp
from jax import lax
from jax.sharding import Mesh
from jax.sharding import PartitionSpec as P

NSEL = 40
XS, CORES, ZS, YS = 4, 2, 8, 4
ROW = ("x", "core")
COL = ("z", "y")
ALL = ("x", "core", "z", "y")
F32 = jnp.float32
BF16 = jnp.bfloat16


def shift(array, axis, size, by):
    return lax.ppermute(array, axis, [(i, (i + by) % size) for i in range(size)])


def direct_ring(array, axis, size):
    return [array] + [shift(array, axis, size, d if d <= size // 2 else d - size) for d in range(1, size)]


def relay_ring(array, axis, size, halved):
    got = [array] + [None] * (size - 1)
    right = left = array
    for step in range(1, size // 2):
        right = shift(right, axis, size, 1)
        left = shift(left, axis, size, -1)
        got[step], got[size - step] = right, left
    if halved:
        half = array.shape[0] // 2
        got[size // 2] = jnp.concatenate(
            [shift(right[:half], axis, size, 1), shift(left[half:], axis, size, -1)], axis=0
        )
    else:
        got[size // 2] = shift(right, axis, size, 1)
    return got


def placed_by_owner(got, own, axis):
    size, width = len(got), got[0].shape[axis]
    dims = list(got[0].shape)
    dims[axis] *= size
    whole = jnp.zeros(dims, got[0].dtype)
    for d, chunk in enumerate(got):
        whole = lax.dynamic_update_slice_in_dim(whole, chunk, (own - d) % size * width, axis)
    return whole


def panel_y_then_z(piece):
    part = placed_by_owner(direct_ring(piece, "y", YS), lax.axis_index("y"), 0)
    return lax.all_gather(part, "z", axis=0, tiled=True)


def batches_of(ring):
    early = jnp.concatenate([ring[d] for d in (2, 1, 0, 7, 6)], axis=0)
    return early, jnp.concatenate([ring[d] for d in (5, 4, 3)], axis=0)


def by_place(early, late):
    z = lax.axis_index("z")
    long = jnp.zeros((ZS + 4, *early.shape[1:]), early.dtype)
    long = lax.dynamic_update_slice_in_dim(long, early, (z - 2) % ZS, 0)
    long = lax.dynamic_update_slice_in_dim(long, late, (z + 3) % ZS, 0)
    return jnp.concatenate([long[:4] + long[ZS:], long[4:ZS]], axis=0)


def device(x, core, z, y):
    return ((x * CORES + core) * ZS + z) * YS + y


def root_of(z):
    return z // CORES, z % CORES


def from_root(array, target):
    pairs = []
    for z in range(ZS):
        for y in range(YS):
            x, core = root_of(z)
            pairs.append((device(x, core, z, y), device(*target(x, core, z, y))))
    return lax.ppermute(array, ALL, pairs)


def along_x(slab, core, shifts):
    return [from_root(slab, lambda x, c, z, y: ((x + by) % XS, core, z, y)) for by in shifts]


def pair_sum(partial):
    first = lax.axis_index("core") == 0
    given = lax.ppermute(jnp.where(first, partial[1], partial[0]), "core", [(0, 1), (1, 0)])
    pair = jnp.where(first, partial[0], partial[1]).astype(F32) + given.astype(F32)
    return pair.astype(BF16)


def sum_over_x(pair):
    x = lax.axis_index("x")
    pair = pair.reshape(XS, -1, pair.shape[1])
    tile = lambda k: lax.dynamic_index_in_dim(pair, (x + k) % XS, 0, keepdims=False)
    opposite = shift(tile(2), "x", XS, 2)
    near = shift(tile(1), "x", XS, 1).astype(F32) + shift(tile(3), "x", XS, -1).astype(F32)
    return (tile(0).astype(F32) + opposite.astype(F32)) + near


def exchanged(array, axis, size, by):
    return lax.ppermute(array, axis, [(i, i ^ by) for i in range(size)])


def summed_over_col(array):
    y = lax.axis_index("y")
    quarters = array.reshape(YS, -1, array.shape[1])
    own = lambda k: lax.dynamic_index_in_dim(quarters, y ^ k, 0, keepdims=False)
    part = own(0).astype(F32)
    for k in range(1, YS):
        part = part + exchanged(own(k), "y", YS, k).astype(F32)
    part = lax.optimization_barrier(part.astype(BF16))
    copies = jnp.broadcast_to(part[None], (ZS, *part.shape))
    part = lax.all_to_all(copies, "z", split_axis=0, concat_axis=0, tiled=True)
    part = lax.optimization_barrier(part.astype(F32).sum(axis=0).astype(BF16))
    whole = jnp.zeros(quarters.shape, BF16)
    for k in range(YS):
        got = part if k == 0 else exchanged(part, "y", YS, k)
        whole = lax.dynamic_update_slice_in_dim(whole, got[None], y ^ k, 0)
    return whole.reshape(array.shape)


def own_slab_of_both(array):
    core = lax.axis_index("core")
    slabs = array.reshape(CORES, -1, array.shape[1])
    kept = lax.dynamic_index_in_dim(slabs, core, 0, keepdims=False)
    given = lax.dynamic_index_in_dim(slabs, 1 - core, 0, keepdims=False)
    got = lax.ppermute(given, "core", [(0, 1), (1, 0)])
    return jnp.stack([jnp.where(core == 0, kept, got), jnp.where(core == 0, got, kept)])


def body(listing, pieces, factor_inv, inverse_block, diag_inv):
    piece_rows, width = pieces.shape[1:]
    row = lax.axis_index(ROW)
    col = lax.axis_index(COL)
    core, z, y = lax.axis_index("core"), lax.axis_index("z"), lax.axis_index("y")
    chosen = listing[:, :NSEL]

    def keep_of(first, count):
        labels = (first + jnp.arange(count, dtype=jnp.int32)) // width
        return jnp.any(chosen[:, :, None] == labels[None, None, :], axis=1).astype(F32)

    own_keep = keep_of((row * ZS * YS + col) * piece_rows, piece_rows)
    normed = jnp.einsum("srk,skj->srj", pieces, factor_inv, preferred_element_type=F32)
    normed = (normed * own_keep[:, :, None]).astype(BF16)
    rows = inverse_block.shape[0]

    def partial_of(panel):
        return jnp.einsum("qj,pq->jp", panel, inverse_block, preferred_element_type=F32).astype(BF16)

    first = core == 0
    runs = [run[:, None] for run in batches_of(relay_ring(normed[1][None], "z", ZS, False))]
    right, left = [[shift(run, "y", YS, by) for run in runs] for by in (1, -1)]
    near = [by_place(*runs), by_place(*right), by_place(*left)]

    deep = rows // (piece_rows * YS)
    of_slab = lambda part, lane: lax.dynamic_slice_in_dim(part, lane * deep, deep, 0)
    far_part = from_root(
        of_slab(near[0], (y + 2) % YS), lambda x, c, z, y: (x, c, z, (y + 2) % YS)
    )
    slab_parts = [of_slab(near[0], y), of_slab(near[1], y), far_part, of_slab(near[2], y)]
    slab_1 = placed_by_owner(slab_parts, y, 1).reshape(rows, width)
    sent_1 = along_x(slab_1, 1, (1, -1, -2))

    panel_0 = panel_y_then_z(normed[0])
    far = by_place(shift(right[0], "y", YS, 1), shift(left[1], "y", YS, -1))
    panel_1 = placed_by_owner([near[0], near[1], far, near[2]], y, 1)
    partial_1 = partial_of(panel_1.reshape(-1, width))
    panel_0, partial_1, slab_1, sent_1[:2] = lax.optimization_barrier(
        (panel_0, partial_1, slab_1, sent_1[:2])
    )
    slab_0 = lax.dynamic_slice_in_dim(panel_0, y * rows, rows, 0)
    sent_0 = along_x(slab_0, 0, (1, -1, 2))
    across = from_root(
        jnp.where(first, slab_1, slab_0), lambda x, c, z, y: (x, 1 - c, z, y)
    )
    partial = [partial_of(panel_0), partial_1]

    home = row == z
    slab = jnp.where(first, slab_0, slab_1)
    factor_slab = jnp.where(home, slab, sum([*sent_0, *sent_1], across))
    pair = lax.optimization_barrier(pair_sum(partial))
    product = sum_over_x(pair)
    col_keep = lax.dynamic_index_in_dim(keep_of(col * rows, rows), core, 0)
    offdiag = lax.optimization_barrier((-(product * col_keep)).astype(BF16))

    term = -jnp.dot(offdiag, factor_slab, preferred_element_type=F32)
    correction = own_slab_of_both(summed_over_col(term.astype(BF16)))
    return (
        own_slab_of_both(offdiag).transpose(0, 2, 1),
        diag_inv + correction.astype(F32).transpose(0, 2, 1),
    )


def solution(mesh):
    torus = Mesh(mesh.devices.reshape(XS, CORES, ZS, YS), ALL)
    return jax.shard_map(
        body,
        mesh=torus,
        in_specs=(P(), P(None, ALL, None), P(), P(COL, ROW), P(None, None, ROW)),
        out_specs=(P(None, COL, ROW), P(None, None, ROW)),
        check_vma=False,
    )
```

```python
import jax
import jax.numpy as jnp
from jax import lax
from jax.sharding import Mesh
from jax.sharding import PartitionSpec as P

NSEL = 40
XS, CORES, ZS, YS = 4, 2, 8, 4
ROW = ("x", "core")
COL = ("z", "y")
ALL = ("x", "core", "z", "y")
F32 = jnp.float32
BF16 = jnp.bfloat16


def shift(array, axis, size, by):
    return lax.ppermute(array, axis, [(i, (i + by) % size) for i in range(size)])


def direct_ring(array, axis, size):
    return [array] + [shift(array, axis, size, d if d <= size // 2 else d - size) for d in range(1, size)]


def relay_ring(array, axis, size, halved):
    got = [array] + [None] * (size - 1)
    right = left = array
    for step in range(1, size // 2):
        right = shift(right, axis, size, 1)
        left = shift(left, axis, size, -1)
        got[step], got[size - step] = right, left
    if halved:
        half = array.shape[0] // 2
        got[size // 2] = jnp.concatenate(
            [shift(right[:half], axis, size, 1), shift(left[half:], axis, size, -1)], axis=0
        )
    else:
        got[size // 2] = shift(right, axis, size, 1)
    return got


def placed_by_owner(got, own, axis):
    size, width = len(got), got[0].shape[axis]
    dims = list(got[0].shape)
    dims[axis] *= size
    whole = jnp.zeros(dims, got[0].dtype)
    for d, chunk in enumerate(got):
        whole = lax.dynamic_update_slice_in_dim(whole, chunk, (own - d) % size * width, axis)
    return whole


def panel_y_then_z(piece):
    part = placed_by_owner(direct_ring(piece, "y", YS), lax.axis_index("y"), 0)
    return lax.all_gather(part, "z", axis=0, tiled=True)


def batches_of(ring):
    early = jnp.concatenate([ring[d] for d in (2, 1, 0, 7, 6)], axis=0)
    return early, jnp.concatenate([ring[d] for d in (5, 4, 3)], axis=0)


def by_place(early, late):
    z = lax.axis_index("z")
    long = jnp.zeros((ZS + 4, *early.shape[1:]), early.dtype)
    long = lax.dynamic_update_slice_in_dim(long, early, (z - 2) % ZS, 0)
    long = lax.dynamic_update_slice_in_dim(long, late, (z + 3) % ZS, 0)
    return jnp.concatenate([long[:4] + long[ZS:], long[4:ZS]], axis=0)


def device(x, core, z, y):
    return ((x * CORES + core) * ZS + z) * YS + y


def root_of(z):
    return z // CORES, z % CORES


def from_root(array, target):
    pairs = []
    for z in range(ZS):
        for y in range(YS):
            x, core = root_of(z)
            pairs.append((device(x, core, z, y), device(*target(x, core, z, y))))
    return lax.ppermute(array, ALL, pairs)


def along_x(slab, core, shifts):
    return [from_root(slab, lambda x, c, z, y: ((x + by) % XS, core, z, y)) for by in shifts]


def pair_sum(partial):
    first = lax.axis_index("core") == 0
    given = lax.ppermute(jnp.where(first, partial[1], partial[0]), "core", [(0, 1), (1, 0)])
    pair = jnp.where(first, partial[0], partial[1]).astype(F32) + given.astype(F32)
    return pair.astype(BF16)


def sum_over_x(pair):
    x = lax.axis_index("x")
    pair = pair.reshape(XS, -1, pair.shape[1])
    tile = lambda k: lax.dynamic_index_in_dim(pair, (x + k) % XS, 0, keepdims=False)
    opposite = shift(tile(2), "x", XS, 2)
    near = shift(tile(1), "x", XS, 1).astype(F32) + shift(tile(3), "x", XS, -1).astype(F32)
    return (tile(0).astype(F32) + opposite.astype(F32)) + near


def exchanged(array, axis, size, by):
    return lax.ppermute(array, axis, [(i, i ^ by) for i in range(size)])


def summed_over_col(array):
    y = lax.axis_index("y")
    quarters = array.reshape(YS, -1, array.shape[1])
    own = lambda k: lax.dynamic_index_in_dim(quarters, y ^ k, 0, keepdims=False)
    part = own(0).astype(F32)
    for k in range(1, YS):
        part = part + exchanged(own(k), "y", YS, k).astype(F32)
    part = lax.optimization_barrier(part.astype(BF16))
    copies = jnp.broadcast_to(part[None], (ZS, *part.shape))
    part = lax.all_to_all(copies, "z", split_axis=0, concat_axis=0, tiled=True)
    part = lax.optimization_barrier(part.astype(F32).sum(axis=0).astype(BF16))
    whole = jnp.zeros(quarters.shape, BF16)
    for k in range(YS):
        got = part if k == 0 else exchanged(part, "y", YS, k)
        whole = lax.dynamic_update_slice_in_dim(whole, got[None], y ^ k, 0)
    return whole.reshape(array.shape)


def own_slab_of_both(array):
    core = lax.axis_index("core")
    slabs = array.reshape(CORES, -1, array.shape[1])
    kept = lax.dynamic_index_in_dim(slabs, core, 0, keepdims=False)
    given = lax.dynamic_index_in_dim(slabs, 1 - core, 0, keepdims=False)
    got = lax.ppermute(given, "core", [(0, 1), (1, 0)])
    return jnp.stack([jnp.where(core == 0, kept, got), jnp.where(core == 0, got, kept)])


def body(listing, pieces, factor_inv, inverse_block, diag_inv):
    piece_rows, width = pieces.shape[1:]
    row = lax.axis_index(ROW)
    col = lax.axis_index(COL)
    core, z, y = lax.axis_index("core"), lax.axis_index("z"), lax.axis_index("y")
    chosen = listing[:, :NSEL]

    def keep_of(first, count):
        labels = (first + jnp.arange(count, dtype=jnp.int32)) // width
        return jnp.any(chosen[:, :, None] == labels[None, None, :], axis=1).astype(F32)

    own_keep = keep_of((row * ZS * YS + col) * piece_rows, piece_rows)
    normed = jnp.einsum("srk,skj->srj", pieces, factor_inv, preferred_element_type=F32)
    normed = (normed * own_keep[:, :, None]).astype(BF16)
    rows = inverse_block.shape[0]

    def partial_of(panel):
        return jnp.einsum("qj,pq->jp", panel, inverse_block, preferred_element_type=F32).astype(BF16)

    first = core == 0
    runs = [run[:, None] for run in batches_of(relay_ring(normed[1][None], "z", ZS, False))]
    right, left = [[shift(run, "y", YS, by) for run in runs] for by in (1, -1)]
    near = [by_place(*runs), by_place(*right), by_place(*left)]

    deep = rows // (piece_rows * YS)
    of_slab = lambda part, lane: lax.dynamic_slice_in_dim(part, lane * deep, deep, 0)
    far_part = from_root(
        of_slab(near[0], (y + 2) % YS), lambda x, c, z, y: (x, c, z, (y + 2) % YS)
    )
    slab_parts = [of_slab(near[0], y), of_slab(near[1], y), far_part, of_slab(near[2], y)]
    slab_1 = placed_by_owner(slab_parts, y, 1).reshape(rows, width)
    sent_1 = along_x(slab_1, 1, (1, -1, -2))

    panel_0 = panel_y_then_z(normed[0])
    far = by_place(shift(right[0], "y", YS, 1), shift(left[1], "y", YS, -1))
    panel_1 = placed_by_owner([near[0], near[1], far, near[2]], y, 1)
    partial_1 = partial_of(panel_1.reshape(-1, width))
    panel_0, partial_1, slab_1, sent_1[:2] = lax.optimization_barrier(
        (panel_0, partial_1, slab_1, sent_1[:2])
    )
    slab_0 = lax.dynamic_slice_in_dim(panel_0, y * rows, rows, 0)
    sent_0 = along_x(slab_0, 0, (1, -1, 2))
    across = from_root(
        jnp.where(first, slab_1, slab_0), lambda x, c, z, y: (x, 1 - c, z, y)
    )
    partial_0, sent_0[:2] = lax.optimization_barrier((partial_of(panel_0), sent_0[:2]))
    partial = [partial_0, partial_1]

    home = row == z
    slab = jnp.where(first, slab_0, slab_1)
    factor_slab = jnp.where(home, slab, sum([*sent_0, *sent_1], across))
    pair = lax.optimization_barrier(pair_sum(partial))
    product = sum_over_x(pair)
    col_keep = lax.dynamic_index_in_dim(keep_of(col * rows, rows), core, 0)
    offdiag = lax.optimization_barrier((-(product * col_keep)).astype(BF16))

    term = -jnp.dot(offdiag, factor_slab, preferred_element_type=F32)
    correction = own_slab_of_both(summed_over_col(term.astype(BF16)))
    return (
        own_slab_of_both(offdiag).transpose(0, 2, 1),
        diag_inv + correction.astype(F32).transpose(0, 2, 1),
    )


def solution(mesh):
    torus = Mesh(mesh.devices.reshape(XS, CORES, ZS, YS), ALL)
    return jax.shard_map(
        body,
        mesh=torus,
        in_specs=(P(), P(None, ALL, None), P(), P(COL, ROW), P(None, None, ROW)),
        out_specs=(P(None, COL, ROW), P(None, None, ROW)),
        check_vma=False,
    )
```

```python
import jax
import jax.numpy as jnp
from jax import lax
from jax.sharding import Mesh
from jax.sharding import PartitionSpec as P

NSEL = 40
XS, CORES, ZS, YS = 4, 2, 8, 4
ROW = ("x", "core")
COL = ("z", "y")
ALL = ("x", "core", "z", "y")
F32 = jnp.float32
BF16 = jnp.bfloat16


def shift(array, axis, size, by):
    return lax.ppermute(array, axis, [(i, (i + by) % size) for i in range(size)])


def direct_ring(array, axis, size):
    return [array] + [shift(array, axis, size, d if d <= size // 2 else d - size) for d in range(1, size)]


def relay_ring(array, axis, size, halved):
    got = [array] + [None] * (size - 1)
    right = left = array
    for step in range(1, size // 2):
        right = shift(right, axis, size, 1)
        left = shift(left, axis, size, -1)
        got[step], got[size - step] = right, left
    if halved:
        half = array.shape[0] // 2
        got[size // 2] = jnp.concatenate(
            [shift(right[:half], axis, size, 1), shift(left[half:], axis, size, -1)], axis=0
        )
    else:
        got[size // 2] = shift(right, axis, size, 1)
    return got


def placed_by_owner(got, own, axis):
    size, width = len(got), got[0].shape[axis]
    dims = list(got[0].shape)
    dims[axis] *= size
    whole = jnp.zeros(dims, got[0].dtype)
    for d, chunk in enumerate(got):
        whole = lax.dynamic_update_slice_in_dim(whole, chunk, (own - d) % size * width, axis)
    return whole


def panel_y_then_z(piece):
    part = placed_by_owner(direct_ring(piece, "y", YS), lax.axis_index("y"), 0)
    return lax.all_gather(part, "z", axis=0, tiled=True)


def near_z_then_y(piece):
    part = placed_by_owner(relay_ring(piece[None], "z", ZS, False), lax.axis_index("z"), 0)[:, None]
    return [part, shift(part, "y", YS, 1), shift(part, "y", YS, -1)]


def far_chunk(near):
    half = near[0].shape[0] // 2
    right = shift(near[1][:half], "y", YS, 1)
    return jnp.concatenate([right, shift(near[2][half:], "y", YS, -1)], axis=0)


def device(x, core, z, y):
    return ((x * CORES + core) * ZS + z) * YS + y


def root_of(z):
    return z // CORES, z % CORES


def from_root(array, target):
    pairs = []
    for z in range(ZS):
        for y in range(YS):
            x, core = root_of(z)
            pairs.append((device(x, core, z, y), device(*target(x, core, z, y))))
    return lax.ppermute(array, ALL, pairs)


def to_ring(tiles, core):
    return [
        from_root(tiles[by], lambda x, c, z, y: ((x + by) % XS, core, z, y)) for by in (1, 2, 3)
    ]


def pair_sum(partial):
    first = lax.axis_index("core") == 0
    given = lax.ppermute(jnp.where(first, partial[1], partial[0]), "core", [(0, 1), (1, 0)])
    pair = jnp.where(first, partial[0], partial[1]).astype(F32) + given.astype(F32)
    return pair.astype(BF16)


def sum_over_x(pair):
    x = lax.axis_index("x")
    pair = pair.reshape(XS, -1, pair.shape[1])
    tile = lambda k: lax.dynamic_index_in_dim(pair, (x + k) % XS, 0, keepdims=False)
    opposite = shift(tile(2), "x", XS, 2)
    near = shift(tile(1), "x", XS, 1).astype(F32) + shift(tile(3), "x", XS, -1).astype(F32)
    return (tile(0).astype(F32) + opposite.astype(F32)) + near


def exchanged(array, axis, size, by):
    return lax.ppermute(array, axis, [(i, i ^ by) for i in range(size)])


def summed_over_col(array):
    y = lax.axis_index("y")
    quarters = array.reshape(YS, -1, array.shape[1])
    own = lambda k: lax.dynamic_index_in_dim(quarters, y ^ k, 0, keepdims=False)
    part = own(0).astype(F32)
    for k in range(1, YS):
        part = part + exchanged(own(k), "y", YS, k).astype(F32)
    part = lax.optimization_barrier(part.astype(BF16))
    copies = jnp.broadcast_to(part[None], (ZS, *part.shape))
    part = lax.all_to_all(copies, "z", split_axis=0, concat_axis=0, tiled=True)
    part = lax.optimization_barrier(part.astype(F32).sum(axis=0).astype(BF16))
    whole = jnp.zeros(quarters.shape, BF16)
    for k in range(YS):
        got = part if k == 0 else exchanged(part, "y", YS, k)
        whole = lax.dynamic_update_slice_in_dim(whole, got[None], y ^ k, 0)
    return whole.reshape(array.shape)


def own_slab_of_both(array):
    core = lax.axis_index("core")
    slabs = array.reshape(CORES, -1, array.shape[1])
    kept = lax.dynamic_index_in_dim(slabs, core, 0, keepdims=False)
    given = lax.dynamic_index_in_dim(slabs, 1 - core, 0, keepdims=False)
    got = lax.ppermute(given, "core", [(0, 1), (1, 0)])
    return jnp.stack([jnp.where(core == 0, kept, got), jnp.where(core == 0, got, kept)])


def body(listing, pieces, factor_inv, inverse_block, diag_inv):
    piece_rows, width = pieces.shape[1:]
    row = lax.axis_index(ROW)
    col = lax.axis_index(COL)
    core, z, y = lax.axis_index("core"), lax.axis_index("z"), lax.axis_index("y")
    chosen = listing[:, :NSEL]

    def keep_of(first, count):
        labels = (first + jnp.arange(count, dtype=jnp.int32)) // width
        return jnp.any(chosen[:, :, None] == labels[None, None, :], axis=1).astype(F32)

    own_keep = keep_of((row * ZS * YS + col) * piece_rows, piece_rows)
    normed = jnp.einsum("srk,skj->srj", pieces, factor_inv, preferred_element_type=F32)
    normed = (normed * own_keep[:, :, None]).astype(BF16)
    rows = inverse_block.shape[0]

    def partial_of(panel):
        return jnp.dot(inverse_block, panel, preferred_element_type=F32).astype(BF16)

    first = core == 0
    near = near_z_then_y(normed[1])

    deep = rows // (piece_rows * YS)
    of_slab = lambda part, lane: lax.dynamic_slice_in_dim(part, lane * deep, deep, 0)
    far_part = from_root(
        of_slab(near[0], (y + 2) % YS), lambda x, c, z, y: (x, c, z, (y + 2) % YS)
    )
    slab_parts = [of_slab(near[0], y), of_slab(near[1], y), far_part, of_slab(near[2], y)]
    slab_1 = placed_by_owner(slab_parts, y, 1).reshape(rows, width)
    x = lax.axis_index("x")
    share = rows // XS
    chip = lambda by: (z // CORES + by) % XS
    tiles_1 = [lax.dynamic_slice_in_dim(slab_1, chip(by) * share, share, 0) for by in range(XS)]
    panel_0 = panel_y_then_z(normed[0])
    panel_0, near, tiles_1 = lax.optimization_barrier((panel_0, near, tiles_1))
    chunks = [near[0], near[1], far_chunk(near), near[2]]
    tiles_0 = [
        lax.dynamic_slice_in_dim(panel_0, y * rows + chip(by) * share, share, 0) for by in range(XS)
    ]
    sent_1, sent_0 = to_ring(tiles_1, 1), to_ring(tiles_0, 0)
    across = from_root(
        jnp.where(first, tiles_1[0], tiles_0[0]), lambda x, c, z, y: (x, 1 - c, z, y)
    )
    partial = [partial_of(panel_0)]

    sent = [*sent_1, *sent_0, across]
    chunks, partial[0], sent = lax.optimization_barrier((chunks, partial[0], sent))
    partial.append(partial_of(placed_by_owner(chunks, y, 1).reshape(panel_0.shape)))

    pair = lax.optimization_barrier(pair_sum(partial))
    product = sum_over_x(pair)
    own_tile = jnp.where(first, tiles_0[0], tiles_1[0])
    factor_tile = sum(sent, jnp.where(row == z, own_tile, jnp.zeros((), BF16)))
    tile_keep = lax.dynamic_index_in_dim(keep_of(col * rows + x * share, share), core, 0)
    offdiag_tile = lax.optimization_barrier((-(product * tile_keep.T)).astype(BF16))

    term = -jnp.einsum("pk,pj->kj", offdiag_tile, factor_tile, preferred_element_type=F32)
    term = sum_over_x(lax.optimization_barrier(term.astype(BF16)))
    correction = own_slab_of_both(summed_over_col(term.astype(BF16)))

    sent_to = lambda by: lax.dynamic_slice_in_dim(
        offdiag_tile, (x + by) % XS * (width // XS), width // XS, 1
    )
    got = [sent_to(0)] + [shift(sent_to(by), "x", XS, by) for by in range(1, XS)]
    offdiag = placed_by_owner(got, x, 0).T
    return (
        own_slab_of_both(offdiag).transpose(0, 2, 1),
        diag_inv + correction.astype(F32).transpose(0, 2, 1),
    )


def solution(mesh):
    torus = Mesh(mesh.devices.reshape(XS, CORES, ZS, YS), ALL)
    return jax.shard_map(
        body,
        mesh=torus,
        in_specs=(P(), P(None, ALL, None), P(), P(COL, ROW), P(None, None, ROW)),
        out_specs=(P(None, COL, ROW), P(None, None, ROW)),
        check_vma=False,
    )
```

```python
import jax
import jax.numpy as jnp
from jax import lax
from jax.sharding import Mesh
from jax.sharding import PartitionSpec as P

NSEL = 40
XS, CORES, ZS, YS = 4, 2, 8, 4
ROW = ("x", "core")
COL = ("z", "y")
ALL = ("x", "core", "z", "y")
F32 = jnp.float32
BF16 = jnp.bfloat16


def shift(array, axis, size, by):
    return lax.ppermute(array, axis, [(i, (i + by) % size) for i in range(size)])


def direct_ring(array, axis, size):
    return [array] + [shift(array, axis, size, d if d <= size // 2 else d - size) for d in range(1, size)]


def relay_ring(array, axis, size, halved):
    got = [array] + [None] * (size - 1)
    right = left = array
    for step in range(1, size // 2):
        right = shift(right, axis, size, 1)
        left = shift(left, axis, size, -1)
        got[step], got[size - step] = right, left
    if halved:
        half = array.shape[0] // 2
        got[size // 2] = jnp.concatenate(
            [shift(right[:half], axis, size, 1), shift(left[half:], axis, size, -1)], axis=0
        )
    else:
        got[size // 2] = shift(right, axis, size, 1)
    return got


def placed_by_owner(got, own, axis):
    size, width = len(got), got[0].shape[axis]
    dims = list(got[0].shape)
    dims[axis] *= size
    whole = jnp.zeros(dims, got[0].dtype)
    for d, chunk in enumerate(got):
        whole = lax.dynamic_update_slice_in_dim(whole, chunk, (own - d) % size * width, axis)
    return whole


def panel_y_then_z(piece):
    part = placed_by_owner(direct_ring(piece, "y", YS), lax.axis_index("y"), 0)
    return lax.all_gather(part, "z", axis=0, tiled=True)


def near_z_then_y(piece):
    part = placed_by_owner(relay_ring(piece[None], "z", ZS, False), lax.axis_index("z"), 0)[:, None]
    return [part, shift(part, "y", YS, 1), shift(part, "y", YS, -1)]


def far_chunk(near):
    half = near[0].shape[0] // 2
    right = shift(near[1][:half], "y", YS, 1)
    return jnp.concatenate([right, shift(near[2][half:], "y", YS, -1)], axis=0)


def device(x, core, z, y):
    return ((x * CORES + core) * ZS + z) * YS + y


def root_of(z):
    return z // CORES, z % CORES


def from_root(array, target):
    pairs = []
    for z in range(ZS):
        for y in range(YS):
            x, core = root_of(z)
            pairs.append((device(x, core, z, y), device(*target(x, core, z, y))))
    return lax.ppermute(array, ALL, pairs)


def along_x(slab, core, shifts):
    return sum(from_root(slab, lambda x, c, z, y: ((x + by) % XS, core, z, y)) for by in shifts)


def pair_sum(partial):
    given = lax.ppermute(partial[0], "core", [(1, 0)]).astype(F32)
    given = given + lax.ppermute(partial[1], "core", [(0, 1)]).astype(F32)
    pair = jnp.where(lax.axis_index("core") == 0, partial[0], partial[1]).astype(F32) + given
    return pair.astype(BF16)


def sum_over_x(pair):
    x = lax.axis_index("x")
    pair = pair.reshape(XS, -1, pair.shape[1])
    tile = lambda k: lax.dynamic_index_in_dim(pair, (x + k) % XS, 0, keepdims=False)
    opposite = shift(tile(2), "x", XS, 2)
    near = shift(tile(1), "x", XS, 1).astype(F32) + shift(tile(3), "x", XS, -1).astype(F32)
    return (tile(0).astype(F32) + opposite.astype(F32)) + near


def exchanged(array, axis, size, by):
    return lax.ppermute(array, axis, [(i, i ^ by) for i in range(size)])


def summed_over_col(array):
    y = lax.axis_index("y")
    quarters = array.reshape(YS, -1, array.shape[1])
    own = lambda k: lax.dynamic_index_in_dim(quarters, y ^ k, 0, keepdims=False)
    part = own(0).astype(F32)
    for k in range(1, YS):
        part = part + exchanged(own(k), "y", YS, k).astype(F32)
    part = lax.optimization_barrier(part.astype(BF16))
    copies = jnp.broadcast_to(part[None], (ZS, *part.shape))
    part = lax.all_to_all(copies, "z", split_axis=0, concat_axis=0, tiled=True)
    part = lax.optimization_barrier(part.astype(F32).sum(axis=0).astype(BF16))
    whole = jnp.zeros(quarters.shape, BF16)
    for k in range(YS):
        got = part if k == 0 else exchanged(part, "y", YS, k)
        whole = lax.dynamic_update_slice_in_dim(whole, got[None], y ^ k, 0)
    return whole.reshape(array.shape)


def own_slab_of_both(array):
    core = lax.axis_index("core")
    slabs = array.reshape(CORES, -1, array.shape[1])
    kept = lax.dynamic_index_in_dim(slabs, core, 0, keepdims=False)
    given = lax.dynamic_index_in_dim(slabs, 1 - core, 0, keepdims=False)
    got = lax.ppermute(given, "core", [(0, 1), (1, 0)])
    return jnp.stack([jnp.where(core == 0, kept, got), jnp.where(core == 0, got, kept)])


def body(listing, pieces, factor_inv, inverse_block, diag_inv):
    piece_rows, width = pieces.shape[1:]
    row = lax.axis_index(ROW)
    col = lax.axis_index(COL)
    core, z, y = lax.axis_index("core"), lax.axis_index("z"), lax.axis_index("y")
    chosen = listing[:, :NSEL]

    def keep_of(first, count):
        labels = (first + jnp.arange(count, dtype=jnp.int32)) // width
        return jnp.any(chosen[:, :, None] == labels[None, None, :], axis=1).astype(F32)

    own_keep = keep_of((row * ZS * YS + col) * piece_rows, piece_rows)
    normed = jnp.einsum("srk,skj->srj", pieces, factor_inv, preferred_element_type=F32)
    normed = (normed * own_keep[:, :, None]).astype(BF16)
    rows = inverse_block.shape[0]

    def partial_of(panel):
        return jnp.einsum("qj,pq->jp", panel, inverse_block, preferred_element_type=F32).astype(BF16)

    first = core == 0
    near = near_z_then_y(normed[1])

    deep = rows // (piece_rows * YS)
    of_slab = lambda part, lane: lax.dynamic_slice_in_dim(part, lane * deep, deep, 0)
    far_part = from_root(
        of_slab(near[0], (y + 2) % YS), lambda x, c, z, y: (x, c, z, (y + 2) % YS)
    )
    slab_parts = [of_slab(near[0], y), of_slab(near[1], y), far_part, of_slab(near[2], y)]
    slab_1 = placed_by_owner(slab_parts, y, 1).reshape(rows, width)
    sent_1 = along_x(slab_1, 1, (1, -1, -2))

    panel_0 = panel_y_then_z(normed[0])
    panel_0, near = lax.optimization_barrier((panel_0, near))
    chunks = [near[0], near[1], far_chunk(near), near[2]]
    slab_0 = lax.dynamic_slice_in_dim(panel_0, y * rows, rows, 0)
    sent_0 = along_x(slab_0, 0, (1, -1, 2))
    partial = [partial_of(panel_0)]

    chunks, partial[0] = lax.optimization_barrier((chunks, partial[0]))
    across = from_root(
        jnp.where(first, slab_1, slab_0), lambda x, c, z, y: (x, 1 - c, z, y)
    )
    partial.append(partial_of(placed_by_owner(chunks, y, 1).reshape(panel_0.shape)))

    home = row == z
    factor_slab = jnp.where(home, jnp.where(first, slab_0, slab_1), sent_0 + sent_1 + across)
    pair, factor_slab = lax.optimization_barrier((pair_sum(partial), factor_slab))
    product = sum_over_x(pair)
    col_keep = lax.dynamic_index_in_dim(keep_of(col * rows, rows), core, 0)
    offdiag = lax.optimization_barrier((-(product * col_keep)).astype(BF16))

    term = -jnp.dot(offdiag, factor_slab, preferred_element_type=F32)
    correction = own_slab_of_both(summed_over_col(term.astype(BF16)))
    return (
        own_slab_of_both(offdiag).transpose(0, 2, 1),
        diag_inv + correction.astype(F32).transpose(0, 2, 1),
    )


def solution(mesh):
    torus = Mesh(mesh.devices.reshape(XS, CORES, ZS, YS), ALL)
    return jax.shard_map(
        body,
        mesh=torus,
        in_specs=(P(), P(None, ALL, None), P(), P(COL, ROW), P(None, None, ROW)),
        out_specs=(P(None, COL, ROW), P(None, None, ROW)),
        check_vma=False,
    )
```
